32 devices in a mesh: batch: 2 (over y), region: 4 (over z), scen: 2 (over x), row: 2 (over core).
Axes of the slice: x: 2, y: 2, z: 4, core: 2. Of those that a mesh axis runs over, the one named last changes fastest.
Arguments:
- kkt_inverse: bfloat16 [4, 1536, 1536], P('region', 'row'), may hold values from -0.25 to 1.25, as said below
- bus_load: bfloat16 [4, 1536, 1024], P('region', None, ('batch', 'scen', 'row')), parts along dimension 2, may hold values from -6 to 6
- bus_limit: float32 [4, 1536], P('region'), may hold values from 0.3 to 3
- copy_local: int32 [4, 128], P('region'), may hold values from 0 to 1535, as said below
- copy_dest: int32 [4, 128], P('region'), may hold values from 0 to 3, as said below
- copy_slot: int32 [4, 128], P('region'), may hold values from 0 to 63, as said below
- copy_key: int32 [4, 128], P('region'), may hold values from 0 to 63
- own_key: int32 [4, 4, 64], P('region'), may hold values from -1 to 63, as said below
Outputs:
- dispatch: float32 [4, 1536, 1024], P('region', None, ('batch', 'scen', 'row')), parts along dimension 2
- scaled_duals: float32 [4, 128, 1024], P('region', None, ('batch', 'scen', 'row')), parts along dimension 2
The draws below stay inside these ranges and needn't reach their ends.
There are 2 independent parts, one for each index of `batch`. The reference program is written for one: setup_inputs(seed, part) draws one part's arguments, and reference() takes and returns one part's arrays. A program takes and returns all parts, laid end to end along the dimension named above; an argument that names none is the same for every part. Nothing has to cross between parts.
Inputs may be any that keep to these rules, and one draw needn't show every extreme that they name: `copy_local`: the 128 local buses of one region's copies are distinct. `copy_dest`: A region sends at most 64 copies to one owner; in every draw one owner receives exactly 64 copies from every region. `copy_slot`: within one region, copies with the same owner have distinct slots. own_key[o, r, s] equals copy_key[r, k] for the copy k of region r with copy_dest o and copy_slot s, and -1 where region r has no such copy. `kkt_inverse`: each matrix has a diagonal of 0.75 to 1.25 and independent off-diagonal entries.
All inputs are finite; a program needn't handle non-finite values.
Results may differ from the reference program's by a relative error of at most 0.0026.
Values may be sent and summed in bfloat16 or wider, within the bound.
No kernel may reach another device: no remote copies, remote signals or barrier semaphores. Data moves between devices by JAX's collectives and lax.ppermute only.
A program may use at most 64 MiB of HBM per device.

```python
import math
import jax
import jax.numpy as jnp
from jax import lax

NB = 1536
KB = 128
GO = 64
ITERS = 3
REGIONS = 4
SCEN = 512
CAP = 64


def build_tables(key):
    key_local = jax.random.fold_in(key, 101)
    key_busy = jax.random.fold_in(key, 202)
    key_pool = jax.random.fold_in(key, 303)
    key_order = jax.random.fold_in(key, 404)
    key_pick = jax.random.fold_in(key, 505)
    key_shuffle = jax.random.fold_in(key, 808)
    region_ids = jnp.arange(REGIONS, dtype=jnp.int32)
    busy_owner = jax.random.randint(key_busy, (), 0, REGIONS).astype(jnp.int32)
    others = ((busy_owner + 1 + jnp.arange(REGIONS - 1, dtype=jnp.int32)) % REGIONS).astype(jnp.int32)
    pool_size = (REGIONS - 1) * CAP

    def one_region(region_index):
        inner = (1 + jax.random.permutation(jax.random.fold_in(key_local, region_index), NB - 2)[:KB - 2]).astype(jnp.int32)
        bus_all = jnp.concatenate([jnp.zeros((1,), jnp.int32), jnp.full((1,), NB - 1, jnp.int32), inner])
        bus_pick = bus_all[jax.random.permutation(jax.random.fold_in(key_shuffle, region_index), KB)]
        forced = (region_index % (REGIONS - 1) * CAP).astype(jnp.int32)
        rest = jax.random.permutation(jax.random.fold_in(key_pool, region_index), pool_size - 1)[:KB - CAP - 1].astype(jnp.int32)
        rest = ((forced + 1 + rest) % pool_size).astype(jnp.int32)
        chosen = jnp.concatenate([forced[None], rest])
        dest_row = jnp.concatenate([jnp.full((CAP,), busy_owner, jnp.int32), others[chosen // CAP]])
        slot_row = jnp.concatenate([jnp.arange(CAP, dtype=jnp.int32), (chosen % CAP).astype(jnp.int32)])
        reorder = jax.random.permutation(jax.random.fold_in(key_order, region_index), KB)
        return (bus_pick, dest_row[reorder], slot_row[reorder])
    bus_table, dest_table, slot_table = jax.vmap(one_region)(region_ids)
    key_table = jax.random.randint(key_pick, (REGIONS, KB), 0, GO).astype(jnp.int32)
    source_ids = jnp.broadcast_to(region_ids[:, None], (REGIONS, KB))
    owner_table = jnp.full((REGIONS, REGIONS, CAP), -1, jnp.int32).at[dest_table, source_ids, slot_table].set(key_table)
    return (bus_table, dest_table, slot_table, key_table, owner_table)


def draw_copy_local(key, part):
    return build_tables(key)[0]


def draw_copy_dest(key, part):
    return build_tables(key)[1]


def draw_copy_slot(key, part):
    return build_tables(key)[2]


def draw_copy_key(key, part):
    return build_tables(key)[3]


def draw_own_key(key, part):
    return build_tables(key)[4]


def draw_kkt_inverse(key, part):
    key_diag = jax.random.fold_in(key, 606)
    key_off = jax.random.fold_in(key, 707)
    diag_vals = jax.random.uniform(key_diag, (REGIONS, NB), jnp.float32, 0.75, 1.25)
    spread = 0.5 / NB ** 0.5
    off_vals = jax.random.normal(key_off, (REGIONS, NB, NB), jnp.float32) * spread
    off_vals = jnp.clip(off_vals, -0.25, 0.25)
    identity = jnp.eye(NB, dtype=jnp.float32)
    whole_matrix = off_vals * (1.0 - identity) + identity * diag_vals[:, :, None]
    return whole_matrix.astype(jnp.bfloat16)


def levels(key, dims, shards, low, largest):
    def one(dim, parts):
        heights = jax.random.uniform(jax.random.fold_in(jax.random.fold_in(key, 6), dim), (parts,), jnp.float32, low / len(shards), largest / len(shards))
        return jnp.repeat(jnp.exp(heights), dims[dim] // parts).reshape((-1,) + (1,) * (len(dims) - dim - 1))

    level = one(*shards[0])
    for cut in shards[1:]:
        level = level * one(*cut)
    return level


def centred(key, extent, scale, limit, split=(), held_as=jnp.bfloat16):
    factor_of = levels(key, extent, split, -0.22, 0.18) if split else 1.0
    array = jax.random.normal(key, extent, jnp.float32) * scale * factor_of
    return jnp.minimum(jnp.maximum(array, -limit), limit).astype(held_as)


def setup_inputs(seed: int = 0, part: int = 0) -> dict:
    arg_keys = jax.random.split(jax.random.key(seed), 9)
    part_keys = jax.random.split(jax.random.fold_in(arg_keys[8], part), 9)
    return {
        "kkt_inverse": draw_kkt_inverse(jax.random.fold_in(arg_keys[8], 71), part),
        "bus_load": centred(part_keys[1], (REGIONS, NB, SCEN), 1.0, 6.0, ((0, 4), (2, 4))),
        "bus_limit": jnp.clip(jnp.exp(math.log(3.0) - 2.3025851 * jax.random.uniform(arg_keys[2], (REGIONS, NB), jnp.float32) ** levels(arg_keys[2], (REGIONS, NB), ((0, 4),), -0.2, 0.2)), 0.3, 3.0),
        "copy_local": draw_copy_local(jax.random.fold_in(arg_keys[8], 71), part),
        "copy_dest": draw_copy_dest(jax.random.fold_in(arg_keys[8], 71), part),
        "copy_slot": draw_copy_slot(jax.random.fold_in(arg_keys[8], 71), part),
        "copy_key": draw_copy_key(jax.random.fold_in(arg_keys[8], 71), part),
        "own_key": draw_own_key(jax.random.fold_in(arg_keys[8], 71), part),
    }


PENALTY = 1.0
PROXIMAL = 0.5


def scatter_region(local_rows, values):
    return jnp.zeros((NB, SCEN), jnp.float32).at[local_rows].add(values)


def gather_region(region_field, local_rows):
    return region_field[local_rows]


def pack_region(row_ids, values):
    return jnp.zeros((REGIONS * CAP, SCEN), jnp.float32).at[row_ids].set(values)


def solve_region(matrix_pair):
    return jnp.dot(matrix_pair[0], matrix_pair[1], preferred_element_type=jnp.float32)


def reference(kkt_inverse, bus_load, bus_limit, copy_local, copy_dest, copy_slot, copy_key, own_key):
    send_rows = (copy_dest * CAP + copy_slot).astype(jnp.int32)
    fixed_keys = jnp.where(own_key >= 0, own_key, GO).astype(jnp.int32)
    owner_ids = jnp.arange(REGIONS, dtype=jnp.int32)[None, :, None]
    seg_ids = (owner_ids * (GO + 1) + jnp.transpose(fixed_keys, (1, 0, 2))).reshape(-1)
    lookup = (copy_dest * (GO + 1) + copy_key).reshape(-1).astype(jnp.int32)
    ones_col = jnp.ones((seg_ids.shape[0],), jnp.float32)
    counts = jax.ops.segment_sum(ones_col, seg_ids, num_segments=REGIONS * (GO + 1))
    dispatch = jnp.zeros((REGIONS, NB, SCEN), jnp.float32)
    dual_vals = jnp.zeros((REGIONS, KB, SCEN), jnp.float32)
    consensus = jnp.zeros((REGIONS, KB, SCEN), jnp.float32)
    for iteration in range(ITERS):
        boundary = jax.vmap(scatter_region)(copy_local, consensus - dual_vals)
        drive_cols = (bus_load.astype(jnp.float32) + PROXIMAL * dispatch + PENALTY * boundary).astype(jnp.bfloat16)
        solved = lax.map(solve_region, (kkt_inverse, drive_cols))
        dispatch = jnp.clip(solved, -bus_limit[:, :, None], bus_limit[:, :, None])
        at_copies = jax.vmap(gather_region)(dispatch, copy_local)
        shared = at_copies + dual_vals
        packed = jax.vmap(pack_region)(send_rows, shared)
        totals = jax.ops.segment_sum(packed.reshape(-1, SCEN), seg_ids, num_segments=REGIONS * (GO + 1))
        averages = totals / jnp.maximum(counts, 1.0)[:, None]
        consensus = averages[lookup].reshape(REGIONS, KB, SCEN)
        dual_vals = dual_vals + at_copies - consensus
    return dispatch, dual_vals
```

```python
import jax
import jax.numpy as jnp
from jax import lax
from jax.sharding import PartitionSpec as P

GO = 64
ITERS = 3
PENALTY = 1.0
PROXIMAL = 0.5
F32 = jnp.float32
BF16 = jnp.bfloat16


def dot32(a, b, precision=None):
    return jnp.dot(a, b, precision=precision, preferred_element_type=F32)


def swap_row(x):
    return lax.ppermute(x, "row", [(0, 1), (1, 0)])


def from_others(x, regions):
    if regions & (regions - 1) == 0 and regions <= 8:
        return [
            lax.ppermute(x, "region", [(i, i ^ s) for i in range(regions)])
            for s in range(1, regions)
        ]
    everyone = lax.all_gather(x, "region", axis=0)
    me = lax.axis_index("region")
    return [
        lax.dynamic_index_in_dim(everyone, lax.rem(me + s, regions), 0, keepdims=False)
        for s in range(1, regions)
    ]


def per_device(
    kkt_inverse, bus_load, bus_limit, copy_local, copy_dest, copy_slot, copy_key, own_key
):
    del copy_slot, own_key
    kh = kkt_inverse[0]
    load = bus_load[0]
    limit = bus_limit[0]
    local_rows = copy_local[0]
    dest = copy_dest[0]
    key = copy_key[0]
    regions = lax.axis_size("region")
    half, buses = kh.shape
    cols = load.shape[1]
    copies = local_rows.shape[0]
    h = lax.axis_index("row")
    first = h * half
    other = half - first

    bus_ids = lax.broadcasted_iota(jnp.int32, (copies, buses), 1)
    picked = local_rows[:, None] == bus_ids
    pick = picked.astype(BF16)
    place = (
        lax.broadcasted_iota(jnp.int32, (buses, copies), 0) == local_rows[None, :]
    ).astype(BF16)
    pick_half = (
        local_rows[:, None] - first == lax.broadcasted_iota(jnp.int32, (copies, half), 1)
    ).astype(BF16)
    keep = 1.0 - jnp.sum(place.astype(F32), axis=1, keepdims=True)

    kc_part = dot32(pick_half, kh).astype(BF16)
    kc_other = swap_row(kc_part)
    ko = swap_row(kh)
    kc = kc_part + kc_other
    load_c = dot32(pick, load)
    limit_c = jnp.sum(jnp.where(picked, limit[None, :], 0.0), axis=1, keepdims=True)
    kcc = dot32(kc, place).astype(BF16)

    id_rows = -(-copies // cols)
    tail = -(-2 * id_rows // 16) * 16
    ids = jnp.stack([dest, key]).astype(BF16)
    ids = jnp.pad(ids, ((0, 0), (0, id_rows * cols - copies))).reshape(2 * id_rows, cols)
    ids = jnp.pad(ids, ((0, tail - 2 * id_rows), (0, 0)))
    own_ids = dest * GO + key

    def half_rows(x, start):
        return lax.dynamic_slice_in_dim(x, start, half, 0)

    starts = (first, other)
    inverse_halves = (kh, ko)
    limit_halves = [half_rows(limit, s)[:, None] for s in starts]
    load_halves = [half_rows(load, s).astype(F32) for s in starts]
    keep_halves = [half_rows(keep, s) for s in starts]

    drive = load
    at = jnp.clip(dot32(kc, load), -limit_c, limit_c)
    dual = jnp.zeros((copies, cols), F32)
    sent = jnp.zeros((copies, cols), F32)
    totals_others = jnp.zeros((copies, cols), F32)
    masks = None
    for iteration in range(ITERS):
        shared = at + dual
        change = (shared - sent).astype(BF16)
        sent = sent + change.astype(F32)
        last = iteration == ITERS - 1
        if iteration == 0:
            arrived = from_others(jnp.concatenate([change, ids], 0), regions)
        else:
            arrived = from_others(change, regions)

        dispatch_halves = [
            jnp.clip(dot32(k, drive), -m, m) for k, m in zip(inverse_halves, limit_halves)
        ]
        if last:
            dispatch = jnp.zeros((buses, cols), F32)
            for s, d in zip(starts, dispatch_halves):
                dispatch = lax.dynamic_update_slice_in_dim(dispatch, d, s, 0)
        else:
            known = jnp.zeros((buses, cols), BF16)
            for s, d, l, k in zip(starts, dispatch_halves, load_halves, keep_halves):
                part = ((l + PROXIMAL * d) * k).astype(BF16)
                known = lax.dynamic_update_slice_in_dim(known, part, s, 0)
            known_c = dot32(kc, known)

        if iteration == 0:
            same = []
            for block in arrived:
                id_block = block[copies:copies + 2 * id_rows].astype(jnp.int32)
                id_block = id_block.reshape(2, id_rows * cols)[:, :copies]
                same.append(own_ids[:, None] == (id_block[0] * GO + id_block[1])[None, :])
            mine = own_ids[:, None] == own_ids[None, :]
            counts = jnp.sum(mine.astype(F32), axis=1, keepdims=True)
            for m in same:
                counts = counts + jnp.sum(m.astype(F32), axis=1, keepdims=True)
            tallies = jnp.maximum(counts, 1.0)
            mine = mine.astype(F32)
            masks = [m.astype(BF16) for m in same]
            arrived = [block[:copies] for block in arrived]
        for m, block in zip(masks, arrived):
            totals_others = totals_others + dot32(m, block)
        totals = dot32(mine, shared, lax.Precision.HIGHEST) + totals_others
        consensus = totals / tallies
        dual = dual + at - consensus
        if not last:
            boundary = consensus - dual
            drive_c = (load_c + PROXIMAL * at + PENALTY * boundary).astype(BF16)
            at = jnp.clip(known_c + dot32(kcc, drive_c), -limit_c, limit_c)
            drive = known + dot32(place, drive_c).astype(BF16)
    return (dispatch[None], dual[None])


def solution(mesh):
    return jax.shard_map(
        per_device,
        mesh=mesh,
        in_specs=(
            P("region", "row", None),
            P("region", None, ("batch", "scen", "row")),
            P("region", None),
            P("region", None),
            P("region", None),
            P("region", None),
            P("region", None),
            P("region", None, None),
        ),
        out_specs=(
            P("region", None, ("batch", "scen", "row")),
            P("region", None, ("batch", "scen", "row")),
        ),
        check_vma=False,
    )
```

```python
import functools

import jax
import jax.numpy as jnp
from jax import lax
from jax.experimental import pallas as pl
from jax.experimental.pallas import tpu as pltpu
from jax.sharding import PartitionSpec as P

GO = 64
ITERS = 3
PENALTY = 1.0
PROXIMAL = 0.5
TAIL = 16
F32 = jnp.float32
BF16 = jnp.bfloat16
VMEM = pl.BlockSpec(memory_space=pltpu.VMEM)


def dot32(a, b, precision=None):
    return jnp.dot(a, b, precision=precision, preferred_element_type=F32)


def in_vmem(body, outs, *operands):
    return pl.pallas_call(
        body,
        out_shape=[pltpu.VMEM(shape, dtype) for shape, dtype in outs],
        in_specs=[VMEM] * len(operands),
        out_specs=[VMEM] * len(outs),
        compiler_params=pltpu.CompilerParams(vmem_limit_bytes=12 << 20),
    )(*[pltpu.with_memory_space_constraint(x, pltpu.VMEM) for x in operands])


def column(row):
    size = row.shape[1]
    return jnp.broadcast_to(row.astype(F32), (size, size)).T


def lanes(shape, offset=0):
    return (lax.broadcasted_iota(jnp.int32, shape, 1) + offset).astype(F32)


def ones_where(condition):
    return jnp.where(condition, 1.0, 0.0).astype(BF16)


def halves(half):
    first = lax.axis_index("row") * half
    return (
        pl.ds(pl.multiple_of(first, half), half),
        pl.ds(pl.multiple_of(half - first, half), half),
    )


def gather_kernel(local_ref, own_ref, part_ref):
    half = own_ref.shape[0]
    wanted = column(local_ref[...]) - (lax.axis_index("row") * half).astype(F32)
    copies = wanted.shape[0]
    pick = jnp.concatenate(
        [ones_where(wanted == lanes(wanted.shape, c)) for c in range(0, half, copies)], 1
    )
    part_ref[...] = dot32(pick, own_ref[...]).astype(BF16)


def tables_kernel(
    local_ref, limit_ref, load_ref, place_ref, bound_ref, keep_ref, load_c_ref, bound_c_ref
):
    buses, cols = load_ref.shape
    local = local_ref[...]
    copies = local.shape[1]
    place = ones_where(lax.broadcasted_iota(jnp.int32, (buses, copies), 0) == local)
    place_ref[...] = place
    keep_ref[...] = 1.0 - dot32(place, jnp.ones((copies, cols), BF16))
    wanted = column(local)
    picks = []
    limits = jnp.zeros((copies, copies), F32)
    for c in range(0, buses, copies):
        limit = limit_ref[:, c:c + copies]
        bound_ref[c:c + copies, :] = jnp.broadcast_to(limit, (cols, copies)).T
        hit = wanted == lanes(wanted.shape, c)
        picks.append(ones_where(hit))
        limits = limits + jnp.where(hit, limit, 0.0)
    load_c_ref[...] = dot32(jnp.concatenate(picks, 1), load_ref[...])
    bound_c_ref[...] = jnp.broadcast_to(jnp.sum(limits, 1, keepdims=True), (copies, cols))


def first_kernel(
    part_ref, other_ref, load_ref, bound_c_ref, dest_ref, key_ref, rows_ref, at_ref, sent_ref,
    message_ref,
):
    rows = (part_ref[...].astype(F32) + other_ref[...].astype(F32)).astype(BF16)
    rows_ref[...] = rows
    bound = bound_c_ref[...]
    at = jnp.clip(dot32(rows, load_ref[...]), -bound, bound)
    at_ref[...] = at
    copies, cols = at.shape
    message = at.astype(BF16)
    sent_ref[...] = message.astype(F32)
    message_ref[:copies, :] = message
    line = lax.broadcasted_iota(jnp.int32, (TAIL, cols), 0)
    ids = jnp.where(line == 0, dest_ref[...], jnp.where(line == 1, key_ref[...], 0))
    message_ref[copies:, :] = ids.astype(F32).astype(BF16)


def own_ids(dest_ref, key_ref):
    return (dest_ref[...] * GO + key_ref[...]).astype(F32)


def own_total(dest_ref, key_ref, shared_ref):
    ids = own_ids(dest_ref, key_ref)
    mine = jnp.where(column(ids) == ids, 1.0, 0.0)
    return dot32(mine, shared_ref[...], lax.Precision.HIGHEST)


def solve_all(own_ref, swapped_ref, drive, bound_ref):
    half = own_ref.shape[0]
    for rows, part_ref in zip(halves(half), (own_ref, swapped_ref)):
        bound = bound_ref[rows, :]
        yield rows, jnp.clip(dot32(part_ref[...], drive), -bound, bound)


def known_part(
    own_ref, swapped_ref, drive, bound_ref, keep_ref, load_ref, rows_ref, known_ref, known_c_ref
):
    for rows, dispatch in solve_all(own_ref, swapped_ref, drive, bound_ref):
        known = (load_ref[rows, :].astype(F32) + PROXIMAL * dispatch) * keep_ref[rows, :]
        known_ref[rows, :] = known.astype(BF16)
    known_c_ref[...] = dot32(rows_ref[...], known_ref[...])


def first_solve_kernel(
    own_ref, swapped_ref, load_ref, bound_ref, keep_ref, rows_ref, place_ref, dest_ref, key_ref,
    shared_ref, known_ref, known_c_ref, block_ref, own_total_ref,
):
    own_total_ref[...] = own_total(dest_ref, key_ref, shared_ref)
    block_ref[...] = dot32(rows_ref[...], place_ref[...]).astype(BF16)
    known_part(
        own_ref, swapped_ref, load_ref[...], bound_ref, keep_ref, load_ref, rows_ref, known_ref,
        known_c_ref,
    )


def drive_of(known_ref, place_ref, drive_c_ref):
    return known_ref[...] + dot32(place_ref[...], drive_c_ref[...]).astype(BF16)


def next_solve_kernel(
    own_ref, swapped_ref, load_ref, bound_ref, keep_ref, rows_ref, place_ref, dest_ref, key_ref,
    shared_ref, before_ref, drive_c_ref, known_ref, known_c_ref, own_total_ref,
):
    own_total_ref[...] = own_total(dest_ref, key_ref, shared_ref)
    drive = drive_of(before_ref, place_ref, drive_c_ref)
    known_part(
        own_ref, swapped_ref, drive, bound_ref, keep_ref, load_ref, rows_ref, known_ref,
        known_c_ref,
    )


def last_solve_kernel(
    own_ref, swapped_ref, bound_ref, place_ref, dest_ref, key_ref, shared_ref, before_ref,
    drive_c_ref, dispatch_ref, own_total_ref,
):
    own_total_ref[...] = own_total(dest_ref, key_ref, shared_ref)
    drive = drive_of(before_ref, place_ref, drive_c_ref)
    for rows, dispatch in solve_all(own_ref, swapped_ref, drive, bound_ref):
        dispatch_ref[rows, :] = dispatch


def advance(
    consensus, dual, at_ref, load_c_ref, bound_c_ref, known_c_ref, block_ref, sent_ref, change_ref,
    drive_c_ref, at_out_ref, dual_out_ref, shared_ref, sent_out_ref,
):
    at = at_ref[...]
    dual = dual + at - consensus
    boundary = consensus - dual
    drive_c = (load_c_ref[...] + PROXIMAL * at + PENALTY * boundary).astype(BF16)
    bound = bound_c_ref[...]
    at = jnp.clip(known_c_ref[...] + dot32(block_ref[...], drive_c), -bound, bound)
    shared = at + dual
    sent = sent_ref[...]
    change = (shared - sent).astype(BF16)
    change_ref[...] = change
    sent_out_ref[...] = sent + change.astype(F32)
    drive_c_ref[...] = drive_c
    at_out_ref[...] = at
    dual_out_ref[...] = dual
    shared_ref[...] = shared


def first_mean_kernel(others, *refs):
    blocks, refs = refs[:others], refs[others:]
    (dest_ref, key_ref, own_total_ref, at_ref, load_c_ref, bound_c_ref, known_c_ref, block_ref,
     sent_ref), refs = refs[:9], refs[9:]
    masks_ref, tally_ref, totals_ref = refs[:3]
    ids = own_ids(dest_ref, key_ref)
    copies = ids.shape[1]
    wanted = column(ids)
    count = jnp.where(wanted == ids, 1.0, 0.0)
    masks = []
    for block in blocks:
        theirs = block[copies:copies + 2, :].astype(F32)
        mask = jnp.where(wanted == theirs[0:1] * GO + theirs[1:2], 1.0, 0.0)
        count = count + mask
        masks.append(mask.astype(BF16))
    mask = jnp.concatenate(masks, 1)
    masks_ref[...] = mask
    tally = jnp.broadcast_to(
        jnp.maximum(jnp.sum(count, 1, keepdims=True), 1.0), tally_ref.shape
    )
    tally_ref[...] = tally
    totals = dot32(mask, jnp.concatenate([block[:copies, :] for block in blocks], 0))
    totals_ref[...] = totals
    consensus = (own_total_ref[...] + totals) / tally
    advance(
        consensus, 0.0, at_ref, load_c_ref, bound_c_ref, known_c_ref, block_ref, sent_ref,
        *refs[3:],
    )


def others_total(blocks, masks_ref, totals_ref):
    arrived = jnp.concatenate([block[...] for block in blocks], 0)
    return totals_ref[...] + dot32(masks_ref[...], arrived)


def next_mean_kernel(others, *refs):
    blocks, refs = refs[:others], refs[others:]
    (masks_ref, tally_ref, totals_ref, dual_ref, own_total_ref, at_ref, load_c_ref, bound_c_ref,
     known_c_ref, block_ref, sent_ref), refs = refs[:11], refs[11:]
    totals = others_total(blocks, masks_ref, totals_ref)
    refs[0][...] = totals
    consensus = (own_total_ref[...] + totals) / tally_ref[...]
    advance(
        consensus, dual_ref[...], at_ref, load_c_ref, bound_c_ref, known_c_ref, block_ref,
        sent_ref, *refs[1:],
    )


def last_mean_kernel(others, *refs):
    blocks, refs = refs[:others], refs[others:]
    masks_ref, tally_ref, totals_ref, dual_ref, own_total_ref, at_ref, out_ref = refs
    totals = others_total(blocks, masks_ref, totals_ref)
    consensus = (own_total_ref[...] + totals) / tally_ref[...]
    out_ref[...] = dual_ref[...] + at_ref[...] - consensus


def swap_row(x):
    return lax.ppermute(x, "row", [(0, 1), (1, 0)])


def from_others(x, regions):
    if regions & (regions - 1) == 0 and regions <= 8:
        return [
            lax.ppermute(x, "region", [(i, i ^ s) for i in range(regions)])
            for s in range(1, regions)
        ]
    everyone = lax.all_gather(x, "region", axis=0)
    me = lax.axis_index("region")
    return [
        lax.dynamic_index_in_dim(everyone, lax.rem(me + s, regions), 0, keepdims=False)
        for s in range(1, regions)
    ]


def per_device(
    kkt_inverse, bus_load, bus_limit, copy_local, copy_dest, copy_slot, copy_key, own_key
):
    del copy_slot, own_key
    own = kkt_inverse[0]
    load = bus_load[0]
    regions = lax.axis_size("region")
    others = regions - 1
    half, buses = own.shape
    cols = load.shape[1]
    copies = copy_local.shape[1]
    small = ((copies, cols), F32)
    small16 = ((copies, cols), BF16)

    (part,) = in_vmem(gather_kernel, [((copies, buses), BF16)], copy_local, own)
    other = swap_row(part)
    swapped = swap_row(own)
    place, bound, keep, load_c, bound_c = in_vmem(
        tables_kernel,
        [((buses, copies), BF16), ((buses, cols), F32), ((buses, cols), F32), small, small],
        copy_local, bus_limit, load,
    )
    rows, at, sent, message = in_vmem(
        first_kernel,
        [((copies, buses), BF16), small, small, ((copies + TAIL, cols), BF16)],
        part, other, load, bound_c, copy_dest, copy_key,
    )
    arrived = from_others(message, regions)
    known, known_c, block, own_sum = in_vmem(
        first_solve_kernel,
        [((buses, cols), BF16), small, ((copies, copies), BF16), small],
        own, swapped, load, bound, keep, rows, place, copy_dest, copy_key, at,
    )
    masks, tally, totals, change, drive_c, at, dual, shared, sent = in_vmem(
        functools.partial(first_mean_kernel, others),
        [((copies, others * copies), BF16), small, small, small16, small16] + [small] * 4,
        *arrived, copy_dest, copy_key, own_sum, at, load_c, bound_c, known_c, block, sent,
    )
    for iteration in range(1, ITERS):
        arrived = from_others(change, regions)
        if iteration < ITERS - 1:
            known, known_c, own_sum = in_vmem(
                next_solve_kernel,
                [((buses, cols), BF16), small, small],
                own, swapped, load, bound, keep, rows, place, copy_dest, copy_key, shared, known,
                drive_c,
            )
            totals, change, drive_c, at, dual, shared, sent = in_vmem(
                functools.partial(next_mean_kernel, others),
                [small, small16, small16] + [small] * 4,
                *arrived, masks, tally, totals, dual, own_sum, at, load_c, bound_c, known_c,
                block, sent,
            )
        else:
            dispatch, own_sum = in_vmem(
                last_solve_kernel,
                [((buses, cols), F32), small],
                own, swapped, bound, place, copy_dest, copy_key, shared, known, drive_c,
            )
            (dual,) = in_vmem(
                functools.partial(last_mean_kernel, others),
                [small],
                *arrived, masks, tally, totals, dual, own_sum, at,
            )
    return (dispatch[None], dual[None])


def solution(mesh):
    return jax.shard_map(
        per_device,
        mesh=mesh,
        in_specs=(
            P("region", "row", None),
            P("region", None, ("batch", "scen", "row")),
            P("region", None),
            P("region", None),
            P("region", None),
            P("region", None),
            P("region", None),
            P("region", None, None),
        ),
        out_specs=(
            P("region", None, ("batch", "scen", "row")),
            P("region", None, ("batch", "scen", "row")),
        ),
        check_vma=False,
    )
```

```python
import functools

import jax
import jax.numpy as jnp
from jax import lax
from jax.experimental import pallas as pl
from jax.experimental.pallas import tpu as pltpu
from jax.sharding import PartitionSpec as P

GO = 64
ITERS = 3
PENALTY = 1.0
PROXIMAL = 0.5
TAIL = 16
F32 = jnp.float32
BF16 = jnp.bfloat16
VMEM = pl.BlockSpec(memory_space=pltpu.VMEM)


def dot32(a, b, precision=None):
    return jnp.dot(a, b, precision=precision, preferred_element_type=F32)


def in_vmem(body, outs, *operands, to_hbm=0, from_hbm=(), scratch=()):
    anywhere = pl.BlockSpec(memory_space=pl.ANY)
    return pl.pallas_call(
        body,
        out_shape=[
            jax.ShapeDtypeStruct(*out) if n < to_hbm else pltpu.VMEM(*out)
            for n, out in enumerate(outs)
        ],
        in_specs=[anywhere] * len(from_hbm) + [VMEM] * len(operands),
        out_specs=[anywhere if n < to_hbm else VMEM for n in range(len(outs))],
        scratch_shapes=list(scratch),
        compiler_params=pltpu.CompilerParams(vmem_limit_bytes=12 << 20),
    )(
        *[pltpu.with_memory_space_constraint(x, pltpu.HBM) for x in from_hbm],
        *[pltpu.with_memory_space_constraint(x, pltpu.VMEM) for x in operands],
    )


def column(row):
    size = row.shape[1]
    return jnp.broadcast_to(row.astype(F32), (size, size)).T


def lanes(shape, offset=0):
    return (lax.broadcasted_iota(jnp.int32, shape, 1) + offset).astype(F32)


def ones_where(condition):
    return jnp.where(condition, 1.0, 0.0).astype(BF16)


def half_starts(half):
    first = lax.axis_index("row") * half
    return first, half - first


def gather_kernel(
    local_hbm, inverse_hbm, limit_hbm, load_hbm, dest_hbm, key_hbm,
    local_ref, own_ref, limit_ref, load_ref, dest_ref, key_ref, part_ref, small_sems, chunk_sems,
):
    half, buses = own_ref.shape
    chunks = chunk_sems.shape[0]
    width = buses // chunks
    first = pltpu.make_async_copy(local_hbm, local_ref, small_sems.at[0])
    first.start()
    pieces = []
    for c in range(chunks):
        columns = slice(c * width, (c + 1) * width)
        pieces.append(
            pltpu.make_async_copy(
                inverse_hbm.at[:, columns], own_ref.at[:, columns], chunk_sems.at[c]
            )
        )
        pieces[c].start()
    rest = [
        pltpu.make_async_copy(source, target, small_sems.at[n + 1])
        for n, (source, target) in enumerate(
            ((load_hbm, load_ref), (limit_hbm, limit_ref), (dest_hbm, dest_ref), (key_hbm, key_ref))
        )
    ]
    for copy in rest:
        copy.start()
    first.wait()
    wanted = column(local_ref[...]) - (lax.axis_index("row") * half).astype(F32)
    copies = wanted.shape[0]
    pick = jnp.concatenate(
        [ones_where(wanted == lanes(wanted.shape, c)) for c in range(0, half, copies)], 1
    )
    for c, piece in enumerate(pieces):
        columns = slice(c * width, (c + 1) * width)
        piece.wait()
        part_ref[:, columns] = dot32(pick, own_ref[:, columns]).astype(BF16)
    for copy in rest:
        copy.wait()


def tables_kernel(
    local_ref, limit_ref, load_ref, place_ref, bound_ref, keep_ref, load_c_ref, bound_c_ref
):
    buses, cols = load_ref.shape
    local = local_ref[...]
    copies = local.shape[1]
    place = ones_where(lax.broadcasted_iota(jnp.int32, (buses, copies), 0) == local)
    place_ref[...] = place
    keep_ref[...] = 1.0 - dot32(place, jnp.ones((copies, cols), BF16))
    wanted = column(local)
    picks = []
    limits = jnp.zeros((copies, copies), F32)
    for c in range(0, buses, copies):
        limit = limit_ref[:, c:c + copies]
        bound_ref[c:c + copies, :] = jnp.broadcast_to(limit, (cols, copies)).T
        hit = wanted == lanes(wanted.shape, c)
        picks.append(ones_where(hit))
        limits = limits + jnp.where(hit, limit, 0.0)
    load_c_ref[...] = dot32(jnp.concatenate(picks, 1), load_ref[...])
    bound_c_ref[...] = jnp.broadcast_to(jnp.sum(limits, 1, keepdims=True), (copies, cols))


def first_kernel(
    part_ref, other_ref, load_ref, bound_c_ref, dest_ref, key_ref, rows_ref, at_ref, sent_ref,
    message_ref,
):
    rows = (part_ref[...].astype(F32) + other_ref[...].astype(F32)).astype(BF16)
    rows_ref[...] = rows
    bound = bound_c_ref[...]
    at = jnp.clip(dot32(rows, load_ref[...]), -bound, bound)
    at_ref[...] = at
    copies, cols = at.shape
    message = at.astype(BF16)
    sent_ref[...] = message.astype(F32)
    message_ref[:copies, :] = message
    line = lax.broadcasted_iota(jnp.int32, (TAIL, cols), 0)
    ids = jnp.where(line == 0, dest_ref[...], jnp.where(line == 1, key_ref[...], 0))
    message_ref[copies:, :] = ids.astype(F32).astype(BF16)


def own_ids(dest_ref, key_ref):
    return (dest_ref[...] * GO + key_ref[...]).astype(F32)


def own_total(dest_ref, key_ref, shared_ref):
    ids = own_ids(dest_ref, key_ref)
    mine = jnp.where(column(ids) == ids, 1.0, 0.0)
    return dot32(mine, shared_ref[...], lax.Precision.HIGHEST)


def solve_all(own_ref, swapped_ref, drive, bound_ref):
    half = own_ref.shape[0]
    quarter = half // 2
    for start, part_ref in zip(half_starts(half), (own_ref, swapped_ref)):
        for step in range(0, half, quarter):
            rows = pl.ds(pl.multiple_of(start + step, quarter), quarter)
            bound = bound_ref[rows, :]
            solved = dot32(part_ref[step:step + quarter, :], drive)
            yield rows, jnp.clip(solved, -bound, bound)


def known_part(
    own_ref, swapped_ref, drive, bound_ref, keep_ref, load_ref, rows_ref, known_ref, known_c_ref
):
    for rows, dispatch in solve_all(own_ref, swapped_ref, drive, bound_ref):
        known = (load_ref[rows, :].astype(F32) + PROXIMAL * dispatch) * keep_ref[rows, :]
        known_ref[rows, :] = known.astype(BF16)
    known_c_ref[...] = dot32(rows_ref[...], known_ref[...])


def first_solve_kernel(
    own_ref, swapped_ref, load_ref, bound_ref, keep_ref, rows_ref, place_ref, dest_ref, key_ref,
    shared_ref, known_ref, known_c_ref, block_ref, own_total_ref,
):
    own_total_ref[...] = own_total(dest_ref, key_ref, shared_ref)
    block_ref[...] = dot32(rows_ref[...], place_ref[...]).astype(BF16)
    known_part(
        own_ref, swapped_ref, load_ref[...], bound_ref, keep_ref, load_ref, rows_ref, known_ref,
        known_c_ref,
    )


def drive_of(known_ref, place_ref, drive_c_ref):
    return known_ref[...] + dot32(place_ref[...], drive_c_ref[...]).astype(BF16)


def next_solve_kernel(
    own_ref, swapped_ref, load_ref, bound_ref, keep_ref, rows_ref, place_ref, dest_ref, key_ref,
    shared_ref, before_ref, drive_c_ref, known_ref, known_c_ref, own_total_ref,
):
    own_total_ref[...] = own_total(dest_ref, key_ref, shared_ref)
    drive = drive_of(before_ref, place_ref, drive_c_ref)
    known_part(
        own_ref, swapped_ref, drive, bound_ref, keep_ref, load_ref, rows_ref, known_ref,
        known_c_ref,
    )


def last_solve_kernel(
    own_ref, swapped_ref, bound_ref, place_ref, dest_ref, key_ref, shared_ref, before_ref,
    drive_c_ref, dispatch_hbm, own_total_ref, dispatch_ref, sems,
):
    drive = drive_of(before_ref, place_ref, drive_c_ref)
    writes = []
    for rows, dispatch in solve_all(own_ref, swapped_ref, drive, bound_ref):
        dispatch_ref[rows, :] = dispatch
        writes.append(
            pltpu.make_async_copy(
                dispatch_ref.at[rows, :], dispatch_hbm.at[rows, :], sems.at[len(writes)]
            )
        )
        writes[-1].start()
    own_total_ref[...] = own_total(dest_ref, key_ref, shared_ref)
    for write in writes:
        write.wait()


def advance(
    consensus, dual, at_ref, load_c_ref, bound_c_ref, known_c_ref, block_ref, sent_ref, change_ref,
    drive_c_ref, at_out_ref, dual_out_ref, shared_ref, *sent_out_ref,
):
    at = at_ref[...]
    dual = dual + at - consensus
    boundary = consensus - dual
    drive_c = (load_c_ref[...] + PROXIMAL * at + PENALTY * boundary).astype(BF16)
    bound = bound_c_ref[...]
    at = jnp.clip(known_c_ref[...] + dot32(block_ref[...], drive_c), -bound, bound)
    shared = at + dual
    sent = sent_ref[...]
    change = (shared - sent).astype(BF16)
    change_ref[...] = change
    for ref in sent_out_ref:
        ref[...] = sent + change.astype(F32)
    drive_c_ref[...] = drive_c
    at_out_ref[...] = at
    dual_out_ref[...] = dual
    shared_ref[...] = shared


def first_mean_kernel(others, *refs):
    blocks, refs = refs[:others], refs[others:]
    (dest_ref, key_ref, own_total_ref, at_ref, load_c_ref, bound_c_ref, known_c_ref, block_ref,
     sent_ref), refs = refs[:9], refs[9:]
    masks_ref, tally_ref, totals_ref = refs[:3]
    ids = own_ids(dest_ref, key_ref)
    copies = ids.shape[1]
    wanted = column(ids)
    count = jnp.where(wanted == ids, 1.0, 0.0)
    masks = []
    for block in blocks:
        theirs = block[copies:copies + 2, :].astype(F32)
        mask = jnp.where(wanted == theirs[0:1] * GO + theirs[1:2], 1.0, 0.0)
        count = count + mask
        masks.append(mask.astype(BF16))
    mask = jnp.concatenate(masks, 1)
    masks_ref[...] = mask
    tally = jnp.broadcast_to(
        jnp.maximum(jnp.sum(count, 1, keepdims=True), 1.0), tally_ref.shape
    )
    tally_ref[...] = tally
    totals = dot32(mask, jnp.concatenate([block[:copies, :] for block in blocks], 0))
    totals_ref[...] = totals
    consensus = (own_total_ref[...] + totals) / tally
    advance(
        consensus, 0.0, at_ref, load_c_ref, bound_c_ref, known_c_ref, block_ref, sent_ref,
        *refs[3:],
    )


def others_total(blocks, masks_ref, totals_ref):
    arrived = jnp.concatenate([block[...] for block in blocks], 0)
    return totals_ref[...] + dot32(masks_ref[...], arrived)


def next_mean_kernel(others, *refs):
    blocks, refs = refs[:others], refs[others:]
    (masks_ref, tally_ref, totals_ref, dual_ref, own_total_ref, at_ref, load_c_ref, bound_c_ref,
     known_c_ref, block_ref, sent_ref), refs = refs[:11], refs[11:]
    totals = others_total(blocks, masks_ref, totals_ref)
    refs[0][...] = totals
    consensus = (own_total_ref[...] + totals) / tally_ref[...]
    advance(
        consensus, dual_ref[...], at_ref, load_c_ref, bound_c_ref, known_c_ref, block_ref,
        sent_ref, *refs[1:],
    )


def last_mean_kernel(others, *refs):
    blocks, refs = refs[:others], refs[others:]
    masks_ref, tally_ref, totals_ref, dual_ref, own_total_ref, at_ref, out_hbm, out_ref, sem = refs
    totals = others_total(blocks, masks_ref, totals_ref)
    consensus = (own_total_ref[...] + totals) / tally_ref[...]
    out_ref[...] = dual_ref[...] + at_ref[...] - consensus
    write = pltpu.make_async_copy(out_ref, out_hbm, sem)
    write.start()
    write.wait()


def swap_row(x):
    return lax.ppermute(x, "row", [(0, 1), (1, 0)])


def from_others(x, regions):
    if regions & (regions - 1) == 0 and regions <= 8:
        return [
            lax.ppermute(x, "region", [(i, i ^ s) for i in range(regions)])
            for s in range(1, regions)
        ]
    everyone = lax.all_gather(x, "region", axis=0)
    me = lax.axis_index("region")
    return [
        lax.dynamic_index_in_dim(everyone, lax.rem(me + s, regions), 0, keepdims=False)
        for s in range(1, regions)
    ]


def consensus_admm(
    kkt_inverse, bus_load, bus_limit, copy_local, copy_dest, copy_slot, copy_key, own_key
):
    del copy_slot, own_key
    own = kkt_inverse[0]
    load = bus_load[0]
    regions = lax.axis_size("region")
    others = regions - 1
    half, buses = own.shape
    cols = load.shape[1]
    copies = copy_local.shape[1]
    small = ((copies, cols), F32)
    small16 = ((copies, cols), BF16)

    local, own, limit, load, dest, key, part = in_vmem(
        gather_kernel,
        [
            (copy_local.shape, jnp.int32), ((half, buses), BF16), (bus_limit.shape, F32),
            ((buses, cols), BF16), (copy_dest.shape, jnp.int32), (copy_key.shape, jnp.int32),
            ((copies, buses), BF16),
        ],
        from_hbm=(copy_local, own, bus_limit, load, copy_dest, copy_key),
        scratch=(pltpu.SemaphoreType.DMA((5,)), pltpu.SemaphoreType.DMA((6,))),
    )
    other = swap_row(part)
    swapped = swap_row(own)
    place, bound, keep, load_c, bound_c = in_vmem(
        tables_kernel,
        [((buses, copies), BF16), ((buses, cols), F32), ((buses, cols), F32), small, small],
        local, limit, load,
    )
    rows, at, sent, message = in_vmem(
        first_kernel,
        [((copies, buses), BF16), small, small, ((copies + TAIL, cols), BF16)],
        part, other, load, bound_c, dest, key,
    )
    arrived = from_others(message, regions)
    known, known_c, block, own_sum = in_vmem(
        first_solve_kernel,
        [((buses, cols), BF16), small, ((copies, copies), BF16), small],
        own, swapped, load, bound, keep, rows, place, dest, key, at,
    )
    masks, tally, totals, change, drive_c, at, dual, shared, sent = in_vmem(
        functools.partial(first_mean_kernel, others),
        [((copies, others * copies), BF16), small, small, small16, small16] + [small] * 4,
        *arrived, dest, key, own_sum, at, load_c, bound_c, known_c, block, sent,
    )
    for iteration in range(1, ITERS):
        arrived = from_others(change, regions)
        if iteration < ITERS - 1:
            known, known_c, own_sum = in_vmem(
                next_solve_kernel,
                [((buses, cols), BF16), small, small],
                own, swapped, load, bound, keep, rows, place, dest, key, shared, known,
                drive_c,
            )
            more = iteration < ITERS - 2
            totals, change, drive_c, at, dual, shared, *kept = in_vmem(
                functools.partial(next_mean_kernel, others),
                [small, small16, small16] + [small] * (4 if more else 3),
                *arrived, masks, tally, totals, dual, own_sum, at, load_c, bound_c, known_c,
                block, sent,
            )
            sent = kept[0] if more else None
        else:
            dispatch, own_sum = in_vmem(
                last_solve_kernel,
                [((buses, cols), F32), small],
                own, swapped, bound, place, dest, key, shared, known, drive_c,
                to_hbm=1,
                scratch=(pltpu.VMEM((buses, cols), F32), pltpu.SemaphoreType.DMA((4,))),
            )
            (dual,) = in_vmem(
                functools.partial(last_mean_kernel, others),
                [small],
                *arrived, masks, tally, totals, dual, own_sum, at,
                to_hbm=1,
                scratch=(pltpu.VMEM((copies, cols), F32), pltpu.SemaphoreType.DMA),
            )
    return (dispatch[None], dual[None])


def solution(mesh):
    return jax.shard_map(
        consensus_admm,
        mesh=mesh,
        in_specs=(
            P("region", "row", None),
            P("region", None, ("batch", "scen", "row")),
            P("region", None),
            P("region", None),
            P("region", None),
            P("region", None),
            P("region", None),
            P("region", None, None),
        ),
        out_specs=(
            P("region", None, ("batch", "scen", "row")),
            P("region", None, ("batch", "scen", "row")),
        ),
        check_vma=False,
    )
```

```python
import functools

import jax
import jax.numpy as jnp
from jax import lax
from jax.experimental import pallas as pl
from jax.experimental.pallas import tpu as pltpu
from jax.sharding import PartitionSpec as P

GO = 64
ITERS = 3
PENALTY = 1.0
PROXIMAL = 0.5
TAIL = 16
F32 = jnp.float32
BF16 = jnp.bfloat16
VMEM = pl.BlockSpec(memory_space=pltpu.VMEM)


def dot32(a, b, precision=None):
    return jnp.dot(a, b, precision=precision, preferred_element_type=F32)


def in_vmem(body, outs, *operands, to_hbm=0, from_hbm=(), scratch=()):
    anywhere = pl.BlockSpec(memory_space=pl.ANY)
    return pl.pallas_call(
        body,
        out_shape=[
            jax.ShapeDtypeStruct(*out) if n < to_hbm else pltpu.VMEM(*out)
            for n, out in enumerate(outs)
        ],
        in_specs=[anywhere] * len(from_hbm) + [VMEM] * len(operands),
        out_specs=[anywhere if n < to_hbm else VMEM for n in range(len(outs))],
        scratch_shapes=list(scratch),
        compiler_params=pltpu.CompilerParams(vmem_limit_bytes=12 << 20),
    )(
        *[pltpu.with_memory_space_constraint(x, pltpu.HBM) for x in from_hbm],
        *[pltpu.with_memory_space_constraint(x, pltpu.VMEM) for x in operands],
    )


def column(row):
    size = row.shape[1]
    return jnp.broadcast_to(row.astype(F32), (size, size)).T


def lanes(shape, offset=0):
    return (lax.broadcasted_iota(jnp.int32, shape, 1) + offset).astype(F32)


def ones_where(condition):
    return jnp.where(condition, 1.0, 0.0).astype(BF16)


def half_starts(half):
    first = lax.axis_index("row") * half
    return first, half - first


def gather_kernel(
    local_hbm, inverse_hbm, limit_hbm, load_hbm, dest_hbm, key_hbm,
    local_ref, own_ref, limit_ref, load_ref, dest_ref, key_ref, part_ref, small_sems, chunk_sems,
):
    copies = local_ref.shape[1]
    first = pltpu.make_async_copy(local_hbm, local_ref, small_sems.at[0])
    first.start()
    pieces = []
    for c in range(chunk_sems.shape[0]):
        block = slice(c * copies, (c + 1) * copies)
        pieces.append(
            pltpu.make_async_copy(inverse_hbm.at[block], own_ref.at[block], chunk_sems.at[c])
        )
        pieces[c].start()
    rest = [
        pltpu.make_async_copy(source, target, small_sems.at[n + 1])
        for n, (source, target) in enumerate(
            ((load_hbm, load_ref), (limit_hbm, limit_ref), (dest_hbm, dest_ref), (key_hbm, key_ref))
        )
    ]
    for copy in rest:
        copy.start()
    first.wait()
    start = lax.axis_index("row") * own_ref.shape[0]
    wanted = column(local_ref[...]) - start.astype(F32)
    found = jnp.zeros(part_ref.shape, F32)
    for c, piece in enumerate(pieces):
        pick = ones_where(wanted == lanes(wanted.shape, c * copies))
        piece.wait()
        found = found + dot32(pick, own_ref[c * copies:(c + 1) * copies, :])
    part_ref[...] = found.astype(BF16)
    for copy in rest:
        copy.wait()


def tables_kernel(
    local_ref, limit_ref, load_ref, place_ref, bound_ref, keep_ref, load_c_ref, bound_c_ref
):
    buses, cols = load_ref.shape
    local = local_ref[...]
    copies = local.shape[1]
    place = ones_where(lax.broadcasted_iota(jnp.int32, (buses, copies), 0) == local)
    place_ref[...] = place
    keep_ref[...] = 1.0 - dot32(place, jnp.ones((copies, cols), BF16))
    wanted = column(local)
    picks = []
    limits = jnp.zeros((copies, copies), F32)
    for c in range(0, buses, copies):
        limit = limit_ref[:, c:c + copies]
        bound_ref[c:c + copies, :] = jnp.broadcast_to(limit, (cols, copies)).T
        hit = wanted == lanes(wanted.shape, c)
        picks.append(ones_where(hit))
        limits = limits + jnp.where(hit, limit, 0.0)
    load_c_ref[...] = dot32(jnp.concatenate(picks, 1), load_ref[...])
    bound_c_ref[...] = jnp.broadcast_to(jnp.sum(limits, 1, keepdims=True), (copies, cols))


def first_kernel(
    part_ref, other_ref, load_ref, bound_c_ref, dest_ref, key_ref, rows_ref, at_ref, sent_ref,
    message_ref,
):
    rows = (part_ref[...].astype(F32) + other_ref[...].astype(F32)).astype(BF16)
    rows_ref[...] = rows
    bound = bound_c_ref[...]
    at = jnp.clip(dot32(rows, load_ref[...]), -bound, bound)
    at_ref[...] = at
    copies, cols = at.shape
    message = at.astype(BF16)
    sent_ref[...] = message.astype(F32)
    message_ref[:copies, :] = message
    line = lax.broadcasted_iota(jnp.int32, (TAIL, cols), 0)
    ids = jnp.where(line == 0, dest_ref[...], jnp.where(line == 1, key_ref[...], 0))
    message_ref[copies:, :] = ids.astype(F32).astype(BF16)


def own_ids(dest_ref, key_ref):
    return (dest_ref[...] * GO + key_ref[...]).astype(F32)


def own_total(dest_ref, key_ref, shared_ref):
    ids = own_ids(dest_ref, key_ref)
    mine = jnp.where(column(ids) == ids, 1.0, 0.0)
    return dot32(mine, shared_ref[...], lax.Precision.HIGHEST)


def solve_all(own_ref, swapped_ref, drive, bound_ref):
    half = own_ref.shape[0]
    quarter = half // 2
    for start, part_ref in zip(half_starts(half), (own_ref, swapped_ref)):
        for step in range(0, half, quarter):
            rows = pl.ds(pl.multiple_of(start + step, quarter), quarter)
            bound = bound_ref[rows, :]
            solved = dot32(part_ref[step:step + quarter, :], drive)
            yield rows, jnp.clip(solved, -bound, bound)


def known_part(
    own_ref, swapped_ref, drive, bound_ref, keep_ref, load_ref, rows_ref, known_ref, known_c_ref
):
    for rows, dispatch in solve_all(own_ref, swapped_ref, drive, bound_ref):
        known = (load_ref[rows, :].astype(F32) + PROXIMAL * dispatch) * keep_ref[rows, :]
        known_ref[rows, :] = known.astype(BF16)
    known_c_ref[...] = dot32(rows_ref[...], known_ref[...])


def first_solve_kernel(
    own_ref, swapped_ref, load_ref, bound_ref, keep_ref, rows_ref, place_ref, dest_ref, key_ref,
    shared_ref, known_ref, known_c_ref, block_ref, own_total_ref,
):
    own_total_ref[...] = own_total(dest_ref, key_ref, shared_ref)
    block_ref[...] = dot32(rows_ref[...], place_ref[...]).astype(BF16)
    known_part(
        own_ref, swapped_ref, load_ref[...], bound_ref, keep_ref, load_ref, rows_ref, known_ref,
        known_c_ref,
    )


def drive_of(known_ref, place_ref, drive_c_ref):
    return known_ref[...] + dot32(place_ref[...], drive_c_ref[...]).astype(BF16)


def next_solve_kernel(
    own_ref, swapped_ref, load_ref, bound_ref, keep_ref, rows_ref, place_ref, dest_ref, key_ref,
    shared_ref, before_ref, drive_c_ref, known_ref, known_c_ref, own_total_ref,
):
    own_total_ref[...] = own_total(dest_ref, key_ref, shared_ref)
    drive = drive_of(before_ref, place_ref, drive_c_ref)
    known_part(
        own_ref, swapped_ref, drive, bound_ref, keep_ref, load_ref, rows_ref, known_ref,
        known_c_ref,
    )


def last_solve_kernel(
    own_ref, swapped_ref, bound_ref, place_ref, dest_ref, key_ref, shared_ref, before_ref,
    drive_c_ref, dispatch_hbm, own_total_ref, dispatch_ref, sems,
):
    drive = drive_of(before_ref, place_ref, drive_c_ref)
    writes = []
    for rows, dispatch in solve_all(own_ref, swapped_ref, drive, bound_ref):
        dispatch_ref[rows, :] = dispatch
        writes.append(
            pltpu.make_async_copy(
                dispatch_ref.at[rows, :], dispatch_hbm.at[rows, :], sems.at[len(writes)]
            )
        )
        writes[-1].start()
    own_total_ref[...] = own_total(dest_ref, key_ref, shared_ref)
    for write in writes:
        write.wait()


def advance(
    consensus, dual, at_ref, load_c_ref, bound_c_ref, known_c_ref, block_ref, sent_ref, change_ref,
    drive_c_ref, at_out_ref, dual_out_ref, shared_ref, *sent_out_ref,
):
    at = at_ref[...]
    dual = dual + at - consensus
    boundary = consensus - dual
    drive_c = (load_c_ref[...] + PROXIMAL * at + PENALTY * boundary).astype(BF16)
    bound = bound_c_ref[...]
    at = jnp.clip(known_c_ref[...] + dot32(block_ref[...], drive_c), -bound, bound)
    shared = at + dual
    sent = sent_ref[...]
    change = (shared - sent).astype(BF16)
    change_ref[...] = change
    for ref in sent_out_ref:
        ref[...] = sent + change.astype(F32)
    drive_c_ref[...] = drive_c
    at_out_ref[...] = at
    dual_out_ref[...] = dual
    shared_ref[...] = shared


def first_mean_kernel(others, *refs):
    blocks, refs = refs[:others], refs[others:]
    (dest_ref, key_ref, own_total_ref, at_ref, load_c_ref, bound_c_ref, known_c_ref, block_ref,
     sent_ref), refs = refs[:9], refs[9:]
    masks_ref, tally_ref, totals_ref = refs[:3]
    ids = own_ids(dest_ref, key_ref)
    copies = ids.shape[1]
    wanted = column(ids)
    count = jnp.where(wanted == ids, 1.0, 0.0)
    masks = []
    for block in blocks:
        theirs = block[copies:copies + 2, :].astype(F32)
        mask = jnp.where(wanted == theirs[0:1] * GO + theirs[1:2], 1.0, 0.0)
        count = count + mask
        masks.append(mask.astype(BF16))
    mask = jnp.concatenate(masks, 1)
    masks_ref[...] = mask
    tally = jnp.broadcast_to(
        jnp.maximum(jnp.sum(count, 1, keepdims=True), 1.0), tally_ref.shape
    )
    tally_ref[...] = tally
    totals = dot32(mask, jnp.concatenate([block[:copies, :] for block in blocks], 0))
    totals_ref[...] = totals
    consensus = (own_total_ref[...] + totals) / tally
    advance(
        consensus, 0.0, at_ref, load_c_ref, bound_c_ref, known_c_ref, block_ref, sent_ref,
        *refs[3:],
    )


def others_total(blocks, masks_ref, totals_ref):
    arrived = jnp.concatenate([block[...] for block in blocks], 0)
    return totals_ref[...] + dot32(masks_ref[...], arrived)


def next_mean_kernel(others, *refs):
    blocks, refs = refs[:others], refs[others:]
    (masks_ref, tally_ref, totals_ref, dual_ref, own_total_ref, at_ref, load_c_ref, bound_c_ref,
     known_c_ref, block_ref, sent_ref), refs = refs[:11], refs[11:]
    totals = others_total(blocks, masks_ref, totals_ref)
    refs[0][...] = totals
    consensus = (own_total_ref[...] + totals) / tally_ref[...]
    advance(
        consensus, dual_ref[...], at_ref, load_c_ref, bound_c_ref, known_c_ref, block_ref,
        sent_ref, *refs[1:],
    )


def last_mean_kernel(others, *refs):
    blocks, refs = refs[:others], refs[others:]
    masks_ref, tally_ref, totals_ref, dual_ref, own_total_ref, at_ref, out_hbm, out_ref, sem = refs
    totals = others_total(blocks, masks_ref, totals_ref)
    consensus = (own_total_ref[...] + totals) / tally_ref[...]
    out_ref[...] = dual_ref[...] + at_ref[...] - consensus
    write = pltpu.make_async_copy(out_ref, out_hbm, sem)
    write.start()
    write.wait()


def swap_row(x):
    return lax.ppermute(x, "row", [(0, 1), (1, 0)])


def from_others(x, regions):
    if regions & (regions - 1) == 0 and regions <= 8:
        return [
            lax.ppermute(x, "region", [(i, i ^ s) for i in range(regions)])
            for s in range(1, regions)
        ]
    everyone = lax.all_gather(x, "region", axis=0)
    me = lax.axis_index("region")
    return [
        lax.dynamic_index_in_dim(everyone, lax.rem(me + s, regions), 0, keepdims=False)
        for s in range(1, regions)
    ]


def consensus_admm(
    kkt_inverse, bus_load, bus_limit, copy_local, copy_dest, copy_slot, copy_key, own_key
):
    del copy_slot, own_key
    own = kkt_inverse[0]
    load = bus_load[0]
    regions = lax.axis_size("region")
    others = regions - 1
    half, buses = own.shape
    cols = load.shape[1]
    copies = copy_local.shape[1]
    small = ((copies, cols), F32)
    small16 = ((copies, cols), BF16)

    local, own, limit, load, dest, key, part = in_vmem(
        gather_kernel,
        [
            (copy_local.shape, jnp.int32), ((half, buses), BF16), (bus_limit.shape, F32),
            ((buses, cols), BF16), (copy_dest.shape, jnp.int32), (copy_key.shape, jnp.int32),
            ((copies, buses), BF16),
        ],
        from_hbm=(copy_local, own, bus_limit, load, copy_dest, copy_key),
        scratch=(pltpu.SemaphoreType.DMA((5,)), pltpu.SemaphoreType.DMA((half // copies,))),
    )
    other = swap_row(part)
    swapped = swap_row(own)
    place, bound, keep, load_c, bound_c = in_vmem(
        tables_kernel,
        [((buses, copies), BF16), ((buses, cols), F32), ((buses, cols), F32), small, small],
        local, limit, load,
    )
    rows, at, sent, message = in_vmem(
        first_kernel,
        [((copies, buses), BF16), small, small, ((copies + TAIL, cols), BF16)],
        part, other, load, bound_c, dest, key,
    )
    arrived = from_others(message, regions)
    known, known_c, block, own_sum = in_vmem(
        first_solve_kernel,
        [((buses, cols), BF16), small, ((copies, copies), BF16), small],
        own, swapped, load, bound, keep, rows, place, dest, key, at,
    )
    masks, tally, totals, change, drive_c, at, dual, shared, sent = in_vmem(
        functools.partial(first_mean_kernel, others),
        [((copies, others * copies), BF16), small, small, small16, small16] + [small] * 4,
        *arrived, dest, key, own_sum, at, load_c, bound_c, known_c, block, sent,
    )
    for iteration in range(1, ITERS):
        arrived = from_others(change, regions)
        if iteration < ITERS - 1:
            known, known_c, own_sum = in_vmem(
                next_solve_kernel,
                [((buses, cols), BF16), small, small],
                own, swapped, load, bound, keep, rows, place, dest, key, shared, known,
                drive_c,
            )
            more = iteration < ITERS - 2
            totals, change, drive_c, at, dual, shared, *kept = in_vmem(
                functools.partial(next_mean_kernel, others),
                [small, small16, small16] + [small] * (4 if more else 3),
                *arrived, masks, tally, totals, dual, own_sum, at, load_c, bound_c, known_c,
                block, sent,
            )
            sent = kept[0] if more else None
        else:
            dispatch, own_sum = in_vmem(
                last_solve_kernel,
                [((buses, cols), F32), small],
                own, swapped, bound, place, dest, key, shared, known, drive_c,
                to_hbm=1,
                scratch=(pltpu.VMEM((buses, cols), F32), pltpu.SemaphoreType.DMA((4,))),
            )
            (dual,) = in_vmem(
                functools.partial(last_mean_kernel, others),
                [small],
                *arrived, masks, tally, totals, dual, own_sum, at,
                to_hbm=1,
                scratch=(pltpu.VMEM((copies, cols), F32), pltpu.SemaphoreType.DMA),
            )
    return (dispatch[None], dual[None])


def solution(mesh):
    return jax.shard_map(
        consensus_admm,
        mesh=mesh,
        in_specs=(
            P("region", "row", None),
            P("region", None, ("batch", "scen", "row")),
            P("region", None),
            P("region", None),
            P("region", None),
            P("region", None),
            P("region", None),
            P("region", None, None),
        ),
        out_specs=(
            P("region", None, ("batch", "scen", "row")),
            P("region", None, ("batch", "scen", "row")),
        ),
        check_vma=False,
    )
```

```python
import functools

import jax
import jax.numpy as jnp
from jax import lax
from jax.experimental import pallas as pl
from jax.experimental.pallas import tpu as pltpu
from jax.sharding import PartitionSpec as P

GO = 64
ITERS = 3
PENALTY = 1.0
PROXIMAL = 0.5
TAIL = 16
F32 = jnp.float32
BF16 = jnp.bfloat16
VMEM = pl.BlockSpec(memory_space=pltpu.VMEM)


def dot32(a, b, precision=None):
    return jnp.dot(a, b, precision=precision, preferred_element_type=F32)


def in_vmem(body, outs, *operands, to_hbm=0, from_hbm=(), scratch=()):
    anywhere = pl.BlockSpec(memory_space=pl.ANY)
    return pl.pallas_call(
        body,
        out_shape=[
            jax.ShapeDtypeStruct(*out) if n < to_hbm else pltpu.VMEM(*out)
            for n, out in enumerate(outs)
        ],
        in_specs=[anywhere] * len(from_hbm) + [VMEM] * len(operands),
        out_specs=[anywhere if n < to_hbm else VMEM for n in range(len(outs))],
        scratch_shapes=list(scratch),
        compiler_params=pltpu.CompilerParams(vmem_limit_bytes=12 << 20),
    )(
        *[pltpu.with_memory_space_constraint(x, pltpu.HBM) for x in from_hbm],
        *[pltpu.with_memory_space_constraint(x, pltpu.VMEM) for x in operands],
    )


def column(row):
    size = row.shape[1]
    return jnp.broadcast_to(row.astype(F32), (size, size)).T


def lanes(shape, offset=0):
    return (lax.broadcasted_iota(jnp.int32, shape, 1) + offset).astype(F32)


def ones_where(condition):
    return jnp.where(condition, 1.0, 0.0).astype(BF16)


def half_starts(half):
    first = lax.axis_index("row") * half
    return first, half - first


def gather_kernel(
    local_hbm, inverse_hbm, limit_hbm, load_hbm, dest_hbm, key_hbm,
    local_ref, own_ref, limit_ref, load_ref, dest_ref, key_ref, part_ref, small_sems, chunk_sems,
):
    copies = local_ref.shape[1]
    first = pltpu.make_async_copy(local_hbm, local_ref, small_sems.at[0])
    first.start()
    pieces = []
    for c in range(chunk_sems.shape[0]):
        block = slice(c * copies, (c + 1) * copies)
        pieces.append(
            pltpu.make_async_copy(inverse_hbm.at[block], own_ref.at[block], chunk_sems.at[c])
        )
        pieces[c].start()
    rest = [
        pltpu.make_async_copy(source, target, small_sems.at[n + 1])
        for n, (source, target) in enumerate(
            ((load_hbm, load_ref), (limit_hbm, limit_ref), (dest_hbm, dest_ref), (key_hbm, key_ref))
        )
    ]
    for copy in rest:
        copy.start()
    first.wait()
    start = lax.axis_index("row") * own_ref.shape[0]
    wanted = column(local_ref[...]) - start.astype(F32)
    found = jnp.zeros(part_ref.shape, F32)
    for c, piece in enumerate(pieces):
        pick = ones_where(wanted == lanes(wanted.shape, c * copies))
        piece.wait()
        found = found + dot32(pick, own_ref[c * copies:(c + 1) * copies, :])
    part_ref[...] = found.astype(BF16)
    for copy in rest:
        copy.wait()


def tables_kernel(
    local_ref, limit_ref, load_ref, place_ref, bound_ref, keep_ref, load_c_ref, bound_c_ref
):
    buses, cols = load_ref.shape
    local = local_ref[...]
    copies = local.shape[1]
    place = ones_where(lax.broadcasted_iota(jnp.int32, (buses, copies), 0) == local)
    place_ref[...] = place
    keep_ref[...] = 1.0 - dot32(place, jnp.ones((copies, cols), BF16))
    wanted = column(local)
    picks = []
    limits = jnp.zeros((copies, copies), F32)
    for c in range(0, buses, copies):
        limit = limit_ref[:, c:c + copies]
        bound_ref[c:c + copies, :] = jnp.broadcast_to(limit, (cols, copies)).T
        hit = wanted == lanes(wanted.shape, c)
        picks.append(ones_where(hit))
        limits = limits + jnp.where(hit, limit, 0.0)
    load_c_ref[...] = dot32(jnp.concatenate(picks, 1), load_ref[...])
    bound_c_ref[...] = jnp.broadcast_to(jnp.sum(limits, 1, keepdims=True), (copies, cols))


def parts_kernel(part_ref, load_ref, load_other_ref, mine_ref, theirs_ref):
    cols = load_ref.shape[1]
    both = dot32(part_ref[...], jnp.concatenate([load_ref[...], load_other_ref[...]], 1))
    mine_ref[...] = both[:, :cols]
    theirs_ref[...] = both[:, cols:]


def first_kernel(
    mine_ref, from_partner_ref, bound_c_ref, dest_ref, key_ref, at_ref, sent_ref, message_ref
):
    bound = bound_c_ref[...]
    at = jnp.clip(mine_ref[...] + from_partner_ref[...], -bound, bound)
    at_ref[...] = at
    copies, cols = at.shape
    message = at.astype(BF16)
    sent_ref[...] = message.astype(F32)
    message_ref[:copies, :] = message
    line = lax.broadcasted_iota(jnp.int32, (TAIL, cols), 0)
    ids = jnp.where(line == 0, dest_ref[...], jnp.where(line == 1, key_ref[...], 0))
    message_ref[copies:, :] = ids.astype(F32).astype(BF16)


def own_ids(dest_ref, key_ref):
    return (dest_ref[...] * GO + key_ref[...]).astype(F32)


def own_total(dest_ref, key_ref, shared_ref):
    ids = own_ids(dest_ref, key_ref)
    mine = jnp.where(column(ids) == ids, 1.0, 0.0)
    return dot32(mine, shared_ref[...], lax.Precision.HIGHEST)


def solve_all(own_ref, swapped_ref, drive, bound_ref):
    half = own_ref.shape[0]
    quarter = half // 2
    for start, part_ref in zip(half_starts(half), (own_ref, swapped_ref)):
        for step in range(0, half, quarter):
            rows = pl.ds(pl.multiple_of(start + step, quarter), quarter)
            bound = bound_ref[rows, :]
            solved = dot32(part_ref[step:step + quarter, :], drive)
            yield rows, jnp.clip(solved, -bound, bound)


def known_part(
    own_ref, swapped_ref, drive, bound_ref, keep_ref, load_ref, rows_ref, known_ref, known_c_ref
):
    for rows, dispatch in solve_all(own_ref, swapped_ref, drive, bound_ref):
        known = (load_ref[rows, :].astype(F32) + PROXIMAL * dispatch) * keep_ref[rows, :]
        known_ref[rows, :] = known.astype(BF16)
    known_c_ref[...] = dot32(rows_ref[...], known_ref[...])


def first_solve_kernel(
    own_ref, swapped_ref, load_ref, bound_ref, keep_ref, part_ref, other_ref, place_ref, dest_ref,
    key_ref, shared_ref, known_ref, known_c_ref, block_ref, own_total_ref, rows_ref,
):
    rows_ref[...] = (part_ref[...].astype(F32) + other_ref[...].astype(F32)).astype(BF16)
    own_total_ref[...] = own_total(dest_ref, key_ref, shared_ref)
    block_ref[...] = dot32(rows_ref[...], place_ref[...]).astype(BF16)
    known_part(
        own_ref, swapped_ref, load_ref[...], bound_ref, keep_ref, load_ref, rows_ref, known_ref,
        known_c_ref,
    )


def drive_of(known_ref, place_ref, drive_c_ref):
    return known_ref[...] + dot32(place_ref[...], drive_c_ref[...]).astype(BF16)


def next_solve_kernel(
    own_ref, swapped_ref, load_ref, bound_ref, keep_ref, rows_ref, place_ref, dest_ref, key_ref,
    shared_ref, before_ref, drive_c_ref, known_ref, known_c_ref, own_total_ref,
):
    own_total_ref[...] = own_total(dest_ref, key_ref, shared_ref)
    drive = drive_of(before_ref, place_ref, drive_c_ref)
    known_part(
        own_ref, swapped_ref, drive, bound_ref, keep_ref, load_ref, rows_ref, known_ref,
        known_c_ref,
    )


def last_solve_kernel(
    own_ref, swapped_ref, bound_ref, place_ref, dest_ref, key_ref, shared_ref, before_ref,
    drive_c_ref, dispatch_hbm, own_total_ref, dispatch_ref, sems,
):
    drive = drive_of(before_ref, place_ref, drive_c_ref)
    writes = []
    for rows, dispatch in solve_all(own_ref, swapped_ref, drive, bound_ref):
        dispatch_ref[rows, :] = dispatch
        writes.append(
            pltpu.make_async_copy(
                dispatch_ref.at[rows, :], dispatch_hbm.at[rows, :], sems.at[len(writes)]
            )
        )
        writes[-1].start()
    own_total_ref[...] = own_total(dest_ref, key_ref, shared_ref)
    for write in writes:
        write.wait()


def advance(
    consensus, dual, at_ref, load_c_ref, bound_c_ref, known_c_ref, block_ref, sent_ref, change_ref,
    drive_c_ref, at_out_ref, dual_out_ref, shared_ref, *sent_out_ref,
):
    at = at_ref[...]
    dual = dual + at - consensus
    boundary = consensus - dual
    drive_c = (load_c_ref[...] + PROXIMAL * at + PENALTY * boundary).astype(BF16)
    bound = bound_c_ref[...]
    at = jnp.clip(known_c_ref[...] + dot32(block_ref[...], drive_c), -bound, bound)
    shared = at + dual
    sent = sent_ref[...]
    change = (shared - sent).astype(BF16)
    change_ref[...] = change
    for ref in sent_out_ref:
        ref[...] = sent + change.astype(F32)
    drive_c_ref[...] = drive_c
    at_out_ref[...] = at
    dual_out_ref[...] = dual
    shared_ref[...] = shared


def first_mean_kernel(others, *refs):
    blocks, refs = refs[:others], refs[others:]
    (dest_ref, key_ref, own_total_ref, at_ref, load_c_ref, bound_c_ref, known_c_ref, block_ref,
     sent_ref), refs = refs[:9], refs[9:]
    masks_ref, tally_ref, totals_ref = refs[:3]
    ids = own_ids(dest_ref, key_ref)
    copies = ids.shape[1]
    wanted = column(ids)
    count = jnp.where(wanted == ids, 1.0, 0.0)
    masks = []
    for block in blocks:
        theirs = block[copies:copies + 2, :].astype(F32)
        mask = jnp.where(wanted == theirs[0:1] * GO + theirs[1:2], 1.0, 0.0)
        count = count + mask
        masks.append(mask.astype(BF16))
    mask = jnp.concatenate(masks, 1)
    masks_ref[...] = mask
    tally = jnp.broadcast_to(
        jnp.maximum(jnp.sum(count, 1, keepdims=True), 1.0), tally_ref.shape
    )
    tally_ref[...] = tally
    totals = dot32(mask, jnp.concatenate([block[:copies, :] for block in blocks], 0))
    totals_ref[...] = totals
    consensus = (own_total_ref[...] + totals) / tally
    advance(
        consensus, 0.0, at_ref, load_c_ref, bound_c_ref, known_c_ref, block_ref, sent_ref,
        *refs[3:],
    )


def others_total(blocks, masks_ref, totals_ref):
    arrived = jnp.concatenate([block[...] for block in blocks], 0)
    return totals_ref[...] + dot32(masks_ref[...], arrived)


def next_mean_kernel(others, *refs):
    blocks, refs = refs[:others], refs[others:]
    (masks_ref, tally_ref, totals_ref, dual_ref, own_total_ref, at_ref, load_c_ref, bound_c_ref,
     known_c_ref, block_ref, sent_ref), refs = refs[:11], refs[11:]
    totals = others_total(blocks, masks_ref, totals_ref)
    refs[0][...] = totals
    consensus = (own_total_ref[...] + totals) / tally_ref[...]
    advance(
        consensus, dual_ref[...], at_ref, load_c_ref, bound_c_ref, known_c_ref, block_ref,
        sent_ref, *refs[1:],
    )


def last_mean_kernel(others, *refs):
    blocks, refs = refs[:others], refs[others:]
    masks_ref, tally_ref, totals_ref, dual_ref, own_total_ref, at_ref, out_hbm, out_ref, sem = refs
    totals = others_total(blocks, masks_ref, totals_ref)
    consensus = (own_total_ref[...] + totals) / tally_ref[...]
    out_ref[...] = dual_ref[...] + at_ref[...] - consensus
    write = pltpu.make_async_copy(out_ref, out_hbm, sem)
    write.start()
    write.wait()


def swap_row(x):
    return lax.ppermute(x, "row", [(0, 1), (1, 0)])


def from_others(x, regions):
    if regions & (regions - 1) == 0 and regions <= 8:
        blocks = []
        for s in range(1, regions):
            swaps = [(i, i ^ s) for i in range(regions)]
            blocks.append(lax.ppermute(x, "region", swaps))
        return blocks
    everyone = lax.all_gather(x, "region", axis=0)
    me = lax.axis_index("region")
    return [
        lax.dynamic_index_in_dim(everyone, lax.rem(me + s, regions), 0, keepdims=False)
        for s in range(1, regions)
    ]


def consensus_admm(
    kkt_inverse, bus_load, bus_limit, copy_local, copy_dest, copy_slot, copy_key, own_key
):
    del copy_slot, own_key
    own = kkt_inverse[0]
    load = bus_load[0]
    regions = lax.axis_size("region")
    others = regions - 1
    half, buses = own.shape
    cols = load.shape[1]
    copies = copy_local.shape[1]
    small = ((copies, cols), F32)
    small16 = ((copies, cols), BF16)

    local, own, limit, load, dest, key, part = in_vmem(
        gather_kernel,
        [
            (copy_local.shape, jnp.int32), ((half, buses), BF16), (bus_limit.shape, F32),
            ((buses, cols), BF16), (copy_dest.shape, jnp.int32), (copy_key.shape, jnp.int32),
            ((copies, buses), BF16),
        ],
        from_hbm=(copy_local, own, bus_limit, load, copy_dest, copy_key),
        scratch=(pltpu.SemaphoreType.DMA((5,)), pltpu.SemaphoreType.DMA((half // copies,))),
    )
    load_other = swap_row(bus_load[0])
    mine, theirs = in_vmem(parts_kernel, [small, small], part, load, load_other)
    from_partner = swap_row(theirs)
    swapped = swap_row(own)
    other = swap_row(part)
    place, bound, keep, load_c, bound_c = in_vmem(
        tables_kernel,
        [((buses, copies), BF16), ((buses, cols), F32), ((buses, cols), F32), small, small],
        local, limit, load,
    )
    at, sent, message = in_vmem(
        first_kernel,
        [small, small, ((copies + TAIL, cols), BF16)],
        mine, from_partner, bound_c, dest, key,
    )
    arrived = from_others(message, regions)
    known, known_c, block, own_sum, rows = in_vmem(
        first_solve_kernel,
        [
            ((buses, cols), BF16), small, ((copies, copies), BF16), small,
            ((copies, buses), BF16),
        ],
        own, swapped, load, bound, keep, part, other, place, dest, key, at,
    )
    masks, tally, totals, change, drive_c, at, dual, shared, sent = in_vmem(
        functools.partial(first_mean_kernel, others),
        [((copies, others * copies), BF16), small, small, small16, small16] + [small] * 4,
        *arrived, dest, key, own_sum, at, load_c, bound_c, known_c, block, sent,
    )
    for iteration in range(1, ITERS):
        arrived = from_others(change, regions)
        if iteration < ITERS - 1:
            known, known_c, own_sum = in_vmem(
                next_solve_kernel,
                [((buses, cols), BF16), small, small],
                own, swapped, load, bound, keep, rows, place, dest, key, shared, known,
                drive_c,
            )
            more = iteration < ITERS - 2
            totals, change, drive_c, at, dual, shared, *kept = in_vmem(
                functools.partial(next_mean_kernel, others),
                [small, small16, small16] + [small] * (4 if more else 3),
                *arrived, masks, tally, totals, dual, own_sum, at, load_c, bound_c, known_c,
                block, sent,
            )
            sent = kept[0] if more else None
        else:
            dispatch, own_sum = in_vmem(
                last_solve_kernel,
                [((buses, cols), F32), small],
                own, swapped, bound, place, dest, key, shared, known, drive_c,
                to_hbm=1,
                scratch=(pltpu.VMEM((buses, cols), F32), pltpu.SemaphoreType.DMA((4,))),
            )
            (dual,) = in_vmem(
                functools.partial(last_mean_kernel, others),
                [small],
                *arrived, masks, tally, totals, dual, own_sum, at,
                to_hbm=1,
                scratch=(pltpu.VMEM((copies, cols), F32), pltpu.SemaphoreType.DMA),
            )
    return (dispatch[None], dual[None])


def solution(mesh):
    return jax.shard_map(
        consensus_admm,
        mesh=mesh,
        in_specs=(
            P("region", "row", None),
            P("region", None, ("batch", "scen", "row")),
            P("region", None),
            P("region", None),
            P("region", None),
            P("region", None),
            P("region", None),
            P("region", None, None),
        ),
        out_specs=(
            P("region", None, ("batch", "scen", "row")),
            P("region", None, ("batch", "scen", "row")),
        ),
        check_vma=False,
    )
```

```python
import functools

import jax
import jax.numpy as jnp
from jax import lax
from jax.experimental import pallas as pl
from jax.experimental.pallas import tpu as pltpu
from jax.sharding import PartitionSpec as P

GO = 64
ITERS = 3
PENALTY = 1.0
PROXIMAL = 0.5
TAIL = 16
F32 = jnp.float32
BF16 = jnp.bfloat16
VMEM = pl.BlockSpec(memory_space=pltpu.VMEM)


def dot32(a, b, precision=None):
    return jnp.dot(a, b, precision=precision, preferred_element_type=F32)


def in_vmem(body, outs, *operands, to_hbm=0, from_hbm=(), scratch=()):
    anywhere = pl.BlockSpec(memory_space=pl.ANY)
    return pl.pallas_call(
        body,
        out_shape=[
            jax.ShapeDtypeStruct(*out) if n < to_hbm else pltpu.VMEM(*out)
            for n, out in enumerate(outs)
        ],
        in_specs=[anywhere] * len(from_hbm) + [VMEM] * len(operands),
        out_specs=[anywhere if n < to_hbm else VMEM for n in range(len(outs))],
        scratch_shapes=list(scratch),
        compiler_params=pltpu.CompilerParams(vmem_limit_bytes=12 << 20),
    )(
        *[pltpu.with_memory_space_constraint(x, pltpu.HBM) for x in from_hbm],
        *[pltpu.with_memory_space_constraint(x, pltpu.VMEM) for x in operands],
    )


def column(row):
    size = row.shape[1]
    return jnp.broadcast_to(row.astype(F32), (size, size)).T


def lanes(shape, offset=0):
    return (lax.broadcasted_iota(jnp.int32, shape, 1) + offset).astype(F32)


def ones_where(condition):
    return jnp.where(condition, 1.0, 0.0).astype(BF16)


def half_starts(half):
    first = lax.axis_index("row") * half
    return first, half - first


def gather_kernel(
    local_hbm, inverse_hbm, limit_hbm, load_hbm, dest_hbm, key_hbm,
    local_ref, own_ref, limit_ref, load_ref, dest_ref, key_ref, part_ref, bound_c_ref,
    small_sems, chunk_sems,
):
    copies = local_ref.shape[1]
    first = [
        pltpu.make_async_copy(local_hbm, local_ref, small_sems.at[0]),
        pltpu.make_async_copy(limit_hbm, limit_ref, small_sems.at[1]),
    ]
    for copy in first:
        copy.start()
    pieces = []
    for c in range(chunk_sems.shape[0]):
        block = slice(c * copies, (c + 1) * copies)
        pieces.append(
            pltpu.make_async_copy(inverse_hbm.at[block], own_ref.at[block], chunk_sems.at[c])
        )
        pieces[c].start()
    rest = [
        pltpu.make_async_copy(source, target, small_sems.at[n + 2])
        for n, (source, target) in enumerate(
            ((load_hbm, load_ref), (dest_hbm, dest_ref), (key_hbm, key_ref))
        )
    ]
    for copy in rest:
        copy.start()
    for copy in first:
        copy.wait()
    wanted = column(local_ref[...])
    limits = jnp.zeros(wanted.shape, F32)
    for c in range(0, limit_ref.shape[1], copies):
        hit = wanted == lanes(wanted.shape, c)
        limits = limits + jnp.where(hit, limit_ref[:, c:c + copies], 0.0)
    bound_c_ref[...] = jnp.broadcast_to(jnp.sum(limits, 1, keepdims=True), bound_c_ref.shape)
    wanted = wanted - (lax.axis_index("row") * own_ref.shape[0]).astype(F32)
    found = jnp.zeros(part_ref.shape, F32)
    for c, piece in enumerate(pieces):
        pick = ones_where(wanted == lanes(wanted.shape, c * copies))
        piece.wait()
        found = found + dot32(pick, own_ref[c * copies:(c + 1) * copies, :])
    part_ref[...] = found.astype(BF16)
    for copy in rest:
        copy.wait()


def tables(local_ref, limit_ref, load_ref, place_ref, bound_ref, keep_ref, load_c_ref):
    buses, cols = load_ref.shape
    local = local_ref[...]
    copies = local.shape[1]
    place = ones_where(lax.broadcasted_iota(jnp.int32, (buses, copies), 0) == local)
    place_ref[...] = place
    keep_ref[...] = 1.0 - dot32(place, jnp.ones((copies, cols), BF16))
    wanted = column(local)
    picks = []
    for c in range(0, buses, copies):
        limit = limit_ref[:, c:c + copies]
        bound_ref[c:c + copies, :] = jnp.broadcast_to(limit, (cols, copies)).T
        picks.append(ones_where(wanted == lanes(wanted.shape, c)))
    load_c_ref[...] = dot32(jnp.concatenate(picks, 1), load_ref[...])


def parts_kernel(part_ref, load_ref, load_other_ref, mine_ref, theirs_ref):
    cols = load_ref.shape[1]
    both = dot32(part_ref[...], jnp.concatenate([load_ref[...], load_other_ref[...]], 1))
    mine_ref[...] = both[:, :cols]
    theirs_ref[...] = both[:, cols:]


def first_kernel(
    mine_ref, from_partner_ref, bound_c_ref, dest_ref, key_ref, at_ref, sent_ref, message_ref
):
    bound = bound_c_ref[...]
    at = jnp.clip(mine_ref[...] + from_partner_ref[...], -bound, bound)
    at_ref[...] = at
    copies, cols = at.shape
    message = at.astype(BF16)
    sent_ref[...] = message.astype(F32)
    message_ref[:copies, :] = message
    line = lax.broadcasted_iota(jnp.int32, (TAIL, cols), 0)
    ids = jnp.where(line == 0, dest_ref[...], jnp.where(line == 1, key_ref[...], 0))
    message_ref[copies:, :] = ids.astype(F32).astype(BF16)


def own_ids(dest_ref, key_ref):
    return (dest_ref[...] * GO + key_ref[...]).astype(F32)


def own_total(dest_ref, key_ref, shared_ref):
    ids = own_ids(dest_ref, key_ref)
    mine = jnp.where(column(ids) == ids, 1.0, 0.0)
    return dot32(mine, shared_ref[...], lax.Precision.HIGHEST)


def solve_all(own_ref, swapped_ref, drive, bound_ref):
    half = own_ref.shape[0]
    quarter = half // 2
    for start, part_ref in zip(half_starts(half), (own_ref, swapped_ref)):
        for step in range(0, half, quarter):
            rows = pl.ds(pl.multiple_of(start + step, quarter), quarter)
            bound = bound_ref[rows, :]
            solved = dot32(part_ref[step:step + quarter, :], drive)
            yield rows, jnp.clip(solved, -bound, bound)


def known_part(
    own_ref, swapped_ref, drive, bound_ref, keep_ref, load_ref, rows_ref, known_ref, known_c_ref
):
    for rows, dispatch in solve_all(own_ref, swapped_ref, drive, bound_ref):
        known = (load_ref[rows, :].astype(F32) + PROXIMAL * dispatch) * keep_ref[rows, :]
        known_ref[rows, :] = known.astype(BF16)
    known_c_ref[...] = dot32(rows_ref[...], known_ref[...])


def first_solve_kernel(
    local_ref, limit_ref, own_ref, swapped_ref, load_ref, part_ref, other_ref, dest_ref, key_ref,
    shared_ref, known_ref, known_c_ref, block_ref, own_total_ref, rows_ref, place_ref, bound_ref,
    keep_ref, load_c_ref, wanted_ref,
):
    tables(local_ref, limit_ref, load_ref, place_ref, bound_ref, keep_ref, load_c_ref)
    rows_ref[...] = (part_ref[...].astype(F32) + other_ref[...].astype(F32)).astype(BF16)
    wanted_ref[...] = column(own_ids(dest_ref, key_ref))
    own_total_ref[...] = own_total(dest_ref, key_ref, shared_ref)
    block_ref[...] = dot32(rows_ref[...], place_ref[...]).astype(BF16)
    known_part(
        own_ref, swapped_ref, load_ref[...], bound_ref, keep_ref, load_ref, rows_ref, known_ref,
        known_c_ref,
    )


def drive_of(known_ref, place_ref, drive_c_ref):
    return known_ref[...] + dot32(place_ref[...], drive_c_ref[...]).astype(BF16)


def next_solve_kernel(
    own_ref, swapped_ref, load_ref, bound_ref, keep_ref, rows_ref, place_ref, dest_ref, key_ref,
    shared_ref, before_ref, drive_c_ref, known_ref, known_c_ref, own_total_ref,
):
    own_total_ref[...] = own_total(dest_ref, key_ref, shared_ref)
    drive = drive_of(before_ref, place_ref, drive_c_ref)
    known_part(
        own_ref, swapped_ref, drive, bound_ref, keep_ref, load_ref, rows_ref, known_ref,
        known_c_ref,
    )


def last_solve_kernel(
    own_ref, swapped_ref, bound_ref, place_ref, dest_ref, key_ref, shared_ref, before_ref,
    drive_c_ref, dispatch_hbm, own_total_ref, dispatch_ref, sems,
):
    drive = drive_of(before_ref, place_ref, drive_c_ref)
    writes = []
    for rows, dispatch in solve_all(own_ref, swapped_ref, drive, bound_ref):
        dispatch_ref[rows, :] = dispatch
        writes.append(
            pltpu.make_async_copy(
                dispatch_ref.at[rows, :], dispatch_hbm.at[rows, :], sems.at[len(writes)]
            )
        )
        writes[-1].start()
    own_total_ref[...] = own_total(dest_ref, key_ref, shared_ref)
    for write in writes:
        write.wait()


def advance(
    consensus, dual, at_ref, load_c_ref, bound_c_ref, known_c_ref, block_ref, sent_ref, change_ref,
    drive_c_ref, at_out_ref, dual_out_ref, shared_ref, *sent_out_ref,
):
    at = at_ref[...]
    dual = dual + at - consensus
    boundary = consensus - dual
    drive_c = (load_c_ref[...] + PROXIMAL * at + PENALTY * boundary).astype(BF16)
    bound = bound_c_ref[...]
    at = jnp.clip(known_c_ref[...] + dot32(block_ref[...], drive_c), -bound, bound)
    shared = at + dual
    sent = sent_ref[...]
    change = (shared - sent).astype(BF16)
    change_ref[...] = change
    for ref in sent_out_ref:
        ref[...] = sent + change.astype(F32)
    drive_c_ref[...] = drive_c
    at_out_ref[...] = at
    dual_out_ref[...] = dual
    shared_ref[...] = shared


def first_mean_kernel(others, *refs):
    blocks, refs = refs[:others], refs[others:]
    (dest_ref, key_ref, wanted_ref, own_total_ref, at_ref, load_c_ref, bound_c_ref, known_c_ref,
     block_ref, sent_ref), refs = refs[:10], refs[10:]
    masks_ref, tally_ref, totals_ref = refs[:3]
    ids = own_ids(dest_ref, key_ref)
    copies = ids.shape[1]
    wanted = wanted_ref[...]
    count = jnp.where(wanted == ids, 1.0, 0.0)
    masks = []
    for block in blocks:
        theirs = block[copies:copies + 2, :].astype(F32)
        mask = jnp.where(wanted == theirs[0:1] * GO + theirs[1:2], 1.0, 0.0)
        count = count + mask
        masks.append(mask.astype(BF16))
    mask = jnp.concatenate(masks, 1)
    masks_ref[...] = mask
    tally = jnp.broadcast_to(
        jnp.maximum(jnp.sum(count, 1, keepdims=True), 1.0), tally_ref.shape
    )
    tally_ref[...] = tally
    totals = dot32(mask, jnp.concatenate([block[:copies, :] for block in blocks], 0))
    totals_ref[...] = totals
    consensus = (own_total_ref[...] + totals) / tally
    advance(
        consensus, 0.0, at_ref, load_c_ref, bound_c_ref, known_c_ref, block_ref, sent_ref,
        *refs[3:],
    )


def others_total(blocks, masks_ref, totals_ref):
    arrived = jnp.concatenate([block[...] for block in blocks], 0)
    return totals_ref[...] + dot32(masks_ref[...], arrived)


def next_mean_kernel(others, *refs):
    blocks, refs = refs[:others], refs[others:]
    (masks_ref, tally_ref, totals_ref, dual_ref, own_total_ref, at_ref, load_c_ref, bound_c_ref,
     known_c_ref, block_ref, sent_ref), refs = refs[:11], refs[11:]
    totals = others_total(blocks, masks_ref, totals_ref)
    refs[0][...] = totals
    consensus = (own_total_ref[...] + totals) / tally_ref[...]
    advance(
        consensus, dual_ref[...], at_ref, load_c_ref, bound_c_ref, known_c_ref, block_ref,
        sent_ref, *refs[1:],
    )


def last_mean_kernel(others, *refs):
    blocks, refs = refs[:others], refs[others:]
    masks_ref, tally_ref, totals_ref, dual_ref, own_total_ref, at_ref, out_hbm, out_ref, sem = refs
    totals = others_total(blocks, masks_ref, totals_ref)
    consensus = (own_total_ref[...] + totals) / tally_ref[...]
    out_ref[...] = dual_ref[...] + at_ref[...] - consensus
    write = pltpu.make_async_copy(out_ref, out_hbm, sem)
    write.start()
    write.wait()


def swap_row(x):
    return lax.ppermute(x, "row", [(0, 1), (1, 0)])


def from_others(x, regions):
    if regions & (regions - 1) == 0 and regions <= 8:
        blocks = []
        for s in range(1, regions):
            swaps = [(i, i ^ s) for i in range(regions)]
            blocks.append(lax.ppermute(x, "region", swaps))
        return blocks
    everyone = lax.all_gather(x, "region", axis=0)
    me = lax.axis_index("region")
    return [
        lax.dynamic_index_in_dim(everyone, lax.rem(me + s, regions), 0, keepdims=False)
        for s in range(1, regions)
    ]


def consensus_admm(
    kkt_inverse, bus_load, bus_limit, copy_local, copy_dest, copy_slot, copy_key, own_key
):
    del copy_slot, own_key
    own = kkt_inverse[0]
    load = bus_load[0]
    regions = lax.axis_size("region")
    others = regions - 1
    half, buses = own.shape
    cols = load.shape[1]
    copies = copy_local.shape[1]
    small = ((copies, cols), F32)
    small16 = ((copies, cols), BF16)

    local, own, limit, load, dest, key, part, bound_c = in_vmem(
        gather_kernel,
        [
            (copy_local.shape, jnp.int32), ((half, buses), BF16), (bus_limit.shape, F32),
            ((buses, cols), BF16), (copy_dest.shape, jnp.int32), (copy_key.shape, jnp.int32),
            ((copies, buses), BF16), small,
        ],
        from_hbm=(copy_local, own, bus_limit, load, copy_dest, copy_key),
        scratch=(pltpu.SemaphoreType.DMA((5,)), pltpu.SemaphoreType.DMA((half // copies,))),
    )
    load_other = swap_row(bus_load[0])
    mine, theirs = in_vmem(parts_kernel, [small, small], part, load, load_other)
    from_partner = swap_row(theirs)
    swapped = swap_row(own)
    other = swap_row(part)
    at, sent, message = in_vmem(
        first_kernel,
        [small, small, ((copies + TAIL, cols), BF16)],
        mine, from_partner, bound_c, dest, key,
    )
    arrived = from_others(message, regions)
    known, known_c, block, own_sum, rows, place, bound, keep, load_c, wanted = in_vmem(
        first_solve_kernel,
        [
            ((buses, cols), BF16), small, ((copies, copies), BF16), small,
            ((copies, buses), BF16), ((buses, copies), BF16), ((buses, cols), F32),
            ((buses, cols), F32), small, ((copies, copies), F32),
        ],
        local, limit, own, swapped, load, part, other, dest, key, at,
    )
    masks, tally, totals, change, drive_c, at, dual, shared, sent = in_vmem(
        functools.partial(first_mean_kernel, others),
        [((copies, others * copies), BF16), small, small, small16, small16] + [small] * 4,
        *arrived, dest, key, wanted, own_sum, at, load_c, bound_c, known_c, block, sent,
    )
    for iteration in range(1, ITERS):
        arrived = from_others(change, regions)
        if iteration < ITERS - 1:
            known, known_c, own_sum = in_vmem(
                next_solve_kernel,
                [((buses, cols), BF16), small, small],
                own, swapped, load, bound, keep, rows, place, dest, key, shared, known,
                drive_c,
            )
            more = iteration < ITERS - 2
            totals, change, drive_c, at, dual, shared, *kept = in_vmem(
                functools.partial(next_mean_kernel, others),
                [small, small16, small16] + [small] * (4 if more else 3),
                *arrived, masks, tally, totals, dual, own_sum, at, load_c, bound_c, known_c,
                block, sent,
            )
            sent = kept[0] if more else None
        else:
            dispatch, own_sum = in_vmem(
                last_solve_kernel,
                [((buses, cols), F32), small],
                own, swapped, bound, place, dest, key, shared, known, drive_c,
                to_hbm=1,
                scratch=(pltpu.VMEM((buses, cols), F32), pltpu.SemaphoreType.DMA((4,))),
            )
            (dual,) = in_vmem(
                functools.partial(last_mean_kernel, others),
                [small],
                *arrived, masks, tally, totals, dual, own_sum, at,
                to_hbm=1,
                scratch=(pltpu.VMEM((copies, cols), F32), pltpu.SemaphoreType.DMA),
            )
    return (dispatch[None], dual[None])


def solution(mesh):
    return jax.shard_map(
        consensus_admm,
        mesh=mesh,
        in_specs=(
            P("region", "row", None),
            P("region", None, ("batch", "scen", "row")),
            P("region", None),
            P("region", None),
            P("region", None),
            P("region", None),
            P("region", None),
            P("region", None, None),
        ),
        out_specs=(
            P("region", None, ("batch", "scen", "row")),
            P("region", None, ("batch", "scen", "row")),
        ),
        check_vma=False,
    )
```

```python
import functools

import jax
import jax.numpy as jnp
from jax import lax
from jax.experimental import pallas as pl
from jax.experimental.pallas import tpu as pltpu
from jax.sharding import PartitionSpec as P

GO = 64
ITERS = 3
PENALTY = 1.0
PROXIMAL = 0.5
TAIL = 16
F32 = jnp.float32
BF16 = jnp.bfloat16
VMEM = pl.BlockSpec(memory_space=pltpu.VMEM)


def dot32(a, b, precision=None):
    return jnp.dot(a, b, precision=precision, preferred_element_type=F32)


def in_vmem(body, outs, *operands, to_hbm=0, from_hbm=(), scratch=()):
    anywhere = pl.BlockSpec(memory_space=pl.ANY)
    return pl.pallas_call(
        body,
        out_shape=[
            jax.ShapeDtypeStruct(*out) if n < to_hbm else pltpu.VMEM(*out)
            for n, out in enumerate(outs)
        ],
        in_specs=[anywhere] * len(from_hbm) + [VMEM] * len(operands),
        out_specs=[anywhere if n < to_hbm else VMEM for n in range(len(outs))],
        scratch_shapes=list(scratch),
        compiler_params=pltpu.CompilerParams(vmem_limit_bytes=12 << 20),
    )(
        *[pltpu.with_memory_space_constraint(x, pltpu.HBM) for x in from_hbm],
        *[pltpu.with_memory_space_constraint(x, pltpu.VMEM) for x in operands],
    )


def column(row):
    size = row.shape[1]
    return jnp.broadcast_to(row.astype(F32), (size, size)).T


def lanes(shape, offset=0):
    return (lax.broadcasted_iota(jnp.int32, shape, 1) + offset).astype(F32)


def ones_where(condition):
    return jnp.where(condition, 1.0, 0.0).astype(BF16)


def half_starts(half):
    first = lax.axis_index("row") * half
    return first, half - first


def gather_kernel(
    local_hbm, inverse_hbm, limit_hbm, load_hbm, dest_hbm, key_hbm,
    local_ref, own_ref, limit_ref, load_ref, dest_ref, key_ref, part_ref, small_sems,
    chunk_sems,
):
    copies = local_ref.shape[1]
    half = own_ref.shape[0]
    size = half // chunk_sems.shape[0]
    first = pltpu.make_async_copy(local_hbm, local_ref, small_sems.at[0])
    first.start()
    pieces = []
    for c in range(chunk_sems.shape[0]):
        block = slice(c * size, (c + 1) * size)
        pieces.append(
            pltpu.make_async_copy(inverse_hbm.at[block], own_ref.at[block], chunk_sems.at[c])
        )
        pieces[c].start()
    rest = [
        pltpu.make_async_copy(source, target, small_sems.at[n + 1])
        for n, (source, target) in enumerate(
            ((load_hbm, load_ref), (limit_hbm, limit_ref), (dest_hbm, dest_ref), (key_hbm, key_ref))
        )
    ]
    for copy in rest:
        copy.start()
    first.wait()
    wanted = column(local_ref[...]) - (lax.axis_index("row") * half).astype(F32)
    found = jnp.zeros(part_ref.shape, BF16)
    for c, piece in enumerate(pieces):
        hits = [
            ones_where(wanted == lanes(wanted.shape, column_start))
            for column_start in range(c * size, (c + 1) * size, copies)
        ]
        piece.wait()
        block = own_ref[c * size:(c + 1) * size, :]
        found = found + dot32(jnp.concatenate(hits, 1), block).astype(BF16)
    part_ref[...] = found
    for copy in rest:
        copy.wait()


def mine_kernel(part_ref, load_ref, local_ref, limit_ref, mine_ref, bound_c_ref):
    mine_ref[...] = dot32(part_ref[...], load_ref[...])
    wanted = column(local_ref[...])
    copies = wanted.shape[0]
    limits = jnp.zeros(wanted.shape, F32)
    for c in range(0, limit_ref.shape[1], copies):
        hit = wanted == lanes(wanted.shape, c)
        limits = limits + jnp.where(hit, limit_ref[:, c:c + copies], 0.0)
    bound_c_ref[...] = jnp.broadcast_to(jnp.sum(limits, 1, keepdims=True), bound_c_ref.shape)


def tables(local_ref, limit_ref, load_ref, place_ref, bound_ref, keep_ref, load_c_ref):
    buses, cols = load_ref.shape
    local = local_ref[...]
    copies = local.shape[1]
    place = ones_where(lax.broadcasted_iota(jnp.int32, (buses, copies), 0) == local)
    place_ref[...] = place
    keep_ref[...] = 1.0 - dot32(place, jnp.ones((copies, cols), BF16))
    wanted = column(local)
    picks = []
    for c in range(0, buses, copies):
        limit = limit_ref[:, c:c + copies]
        bound_ref[c:c + copies, :] = jnp.broadcast_to(limit, (cols, copies)).T
        picks.append(ones_where(wanted == lanes(wanted.shape, c)))
    load_c_ref[...] = dot32(jnp.concatenate(picks, 1), load_ref[...])


def theirs_kernel(part_ref, load_other_ref, theirs_ref):
    theirs_ref[...] = dot32(part_ref[...], load_other_ref[...])


def first_kernel(
    mine_ref, from_partner_ref, bound_c_ref, dest_ref, key_ref, at_ref, sent_ref, message_ref
):
    bound = bound_c_ref[...]
    at = jnp.clip(mine_ref[...] + from_partner_ref[...], -bound, bound)
    at_ref[...] = at
    copies, cols = at.shape
    message = at.astype(BF16)
    sent_ref[...] = message.astype(F32)
    message_ref[:copies, :] = message
    line = lax.broadcasted_iota(jnp.int32, (TAIL, cols), 0)
    ids = jnp.where(line == 0, dest_ref[...], jnp.where(line == 1, key_ref[...], 0))
    message_ref[copies:, :] = ids.astype(F32).astype(BF16)


def own_ids(dest_ref, key_ref):
    return (dest_ref[...] * GO + key_ref[...]).astype(F32)


def own_total(dest_ref, key_ref, shared_ref):
    ids = own_ids(dest_ref, key_ref)
    mine = jnp.where(column(ids) == ids, 1.0, 0.0)
    return dot32(mine, shared_ref[...], lax.Precision.HIGHEST)


def solve_all(own_ref, swapped_ref, drive, bound_ref):
    half = own_ref.shape[0]
    quarter = half // 2
    for start, part_ref in zip(half_starts(half), (own_ref, swapped_ref)):
        for step in range(0, half, quarter):
            rows = pl.ds(pl.multiple_of(start + step, quarter), quarter)
            bound = bound_ref[rows, :]
            solved = dot32(part_ref[step:step + quarter, :], drive)
            yield rows, jnp.clip(solved, -bound, bound)


def known_part(
    own_ref, swapped_ref, drive, bound_ref, keep_ref, load_ref, rows_ref, known_ref, known_c_ref
):
    for rows, dispatch in solve_all(own_ref, swapped_ref, drive, bound_ref):
        known = (load_ref[rows, :].astype(F32) + PROXIMAL * dispatch) * keep_ref[rows, :]
        known_ref[rows, :] = known.astype(BF16)
    known_c_ref[...] = dot32(rows_ref[...], known_ref[...])


def first_solve_kernel(
    local_ref, limit_ref, own_ref, swapped_ref, load_ref, part_ref, other_ref, dest_ref, key_ref,
    shared_ref, known_ref, known_c_ref, block_ref, own_total_ref, rows_ref, place_ref, bound_ref,
    keep_ref, load_c_ref, wanted_ref,
):
    tables(local_ref, limit_ref, load_ref, place_ref, bound_ref, keep_ref, load_c_ref)
    rows_ref[...] = (part_ref[...].astype(F32) + other_ref[...].astype(F32)).astype(BF16)
    wanted_ref[...] = column(own_ids(dest_ref, key_ref))
    own_total_ref[...] = own_total(dest_ref, key_ref, shared_ref)
    block_ref[...] = dot32(rows_ref[...], place_ref[...]).astype(BF16)
    known_part(
        own_ref, swapped_ref, load_ref[...], bound_ref, keep_ref, load_ref, rows_ref, known_ref,
        known_c_ref,
    )


def drive_of(known_ref, place_ref, drive_c_ref):
    return known_ref[...] + dot32(place_ref[...], drive_c_ref[...]).astype(BF16)


def next_solve_kernel(
    own_ref, swapped_ref, load_ref, bound_ref, keep_ref, rows_ref, place_ref, dest_ref, key_ref,
    shared_ref, before_ref, drive_c_ref, known_ref, known_c_ref, own_total_ref,
):
    own_total_ref[...] = own_total(dest_ref, key_ref, shared_ref)
    drive = drive_of(before_ref, place_ref, drive_c_ref)
    known_part(
        own_ref, swapped_ref, drive, bound_ref, keep_ref, load_ref, rows_ref, known_ref,
        known_c_ref,
    )


def last_solve_kernel(
    own_ref, swapped_ref, bound_ref, place_ref, dest_ref, key_ref, shared_ref, before_ref,
    drive_c_ref, dispatch_hbm, own_total_ref, dispatch_ref, sems,
):
    drive = drive_of(before_ref, place_ref, drive_c_ref)
    writes = []
    for rows, dispatch in solve_all(own_ref, swapped_ref, drive, bound_ref):
        dispatch_ref[rows, :] = dispatch
        writes.append(
            pltpu.make_async_copy(
                dispatch_ref.at[rows, :], dispatch_hbm.at[rows, :], sems.at[len(writes)]
            )
        )
        writes[-1].start()
    own_total_ref[...] = own_total(dest_ref, key_ref, shared_ref)
    for write in writes:
        write.wait()


def advance(
    consensus, dual, at_ref, load_c_ref, bound_c_ref, known_c_ref, block_ref, sent_ref, change_ref,
    drive_c_ref, at_out_ref, dual_out_ref, shared_ref, *sent_out_ref,
):
    at = at_ref[...]
    dual = dual + at - consensus
    boundary = consensus - dual
    drive_c = (load_c_ref[...] + PROXIMAL * at + PENALTY * boundary).astype(BF16)
    bound = bound_c_ref[...]
    at = jnp.clip(known_c_ref[...] + dot32(block_ref[...], drive_c), -bound, bound)
    shared = at + dual
    sent = sent_ref[...]
    change = (shared - sent).astype(BF16)
    change_ref[...] = change
    for ref in sent_out_ref:
        ref[...] = sent + change.astype(F32)
    drive_c_ref[...] = drive_c
    at_out_ref[...] = at
    dual_out_ref[...] = dual
    shared_ref[...] = shared


def first_mean_kernel(others, *refs):
    blocks, refs = refs[:others], refs[others:]
    (dest_ref, key_ref, wanted_ref, own_total_ref, at_ref, load_c_ref, bound_c_ref, known_c_ref,
     block_ref, sent_ref), refs = refs[:10], refs[10:]
    masks_ref, share_ref, totals_ref = refs[:3]
    ids = own_ids(dest_ref, key_ref)
    copies = ids.shape[1]
    wanted = wanted_ref[...]
    count = jnp.where(wanted == ids, 1.0, 0.0)
    masks = []
    for block in blocks:
        theirs = block[copies:copies + 2, :].astype(F32)
        mask = jnp.where(wanted == theirs[0:1] * GO + theirs[1:2], 1.0, 0.0)
        count = count + mask
        masks.append(mask.astype(BF16))
    mask = jnp.concatenate(masks, 1)
    masks_ref[...] = mask
    share = 1.0 / jnp.maximum(jnp.sum(count, 1, keepdims=True), 1.0)
    share = jnp.broadcast_to(share, share_ref.shape)
    share_ref[...] = share
    totals = dot32(mask, jnp.concatenate([block[:copies, :] for block in blocks], 0))
    totals_ref[...] = totals
    consensus = (own_total_ref[...] + totals) * share
    advance(
        consensus, 0.0, at_ref, load_c_ref, bound_c_ref, known_c_ref, block_ref, sent_ref,
        *refs[3:],
    )


def others_total(blocks, masks_ref, totals_ref):
    arrived = jnp.concatenate([block[...] for block in blocks], 0)
    return totals_ref[...] + dot32(masks_ref[...], arrived)


def next_mean_kernel(others, *refs):
    blocks, refs = refs[:others], refs[others:]
    (masks_ref, share_ref, totals_ref, dual_ref, own_total_ref, at_ref, load_c_ref, bound_c_ref,
     known_c_ref, block_ref, sent_ref), refs = refs[:11], refs[11:]
    totals = others_total(blocks, masks_ref, totals_ref)
    refs[0][...] = totals
    consensus = (own_total_ref[...] + totals) * share_ref[...]
    advance(
        consensus, dual_ref[...], at_ref, load_c_ref, bound_c_ref, known_c_ref, block_ref,
        sent_ref, *refs[1:],
    )


def last_mean_kernel(others, *refs):
    blocks, refs = refs[:others], refs[others:]
    masks_ref, share_ref, totals_ref, dual_ref, own_total_ref, at_ref, out_hbm, out_ref, sem = refs
    totals = others_total(blocks, masks_ref, totals_ref)
    consensus = (own_total_ref[...] + totals) * share_ref[...]
    out_ref[...] = dual_ref[...] + at_ref[...] - consensus
    write = pltpu.make_async_copy(out_ref, out_hbm, sem)
    write.start()
    write.wait()


def swap_row(x):
    return lax.ppermute(x, "row", [(0, 1), (1, 0)])


def from_others(x, regions):
    if regions & (regions - 1) == 0 and regions <= 8:
        blocks = []
        for s in range(1, regions):
            swaps = [(i, i ^ s) for i in range(regions)]
            blocks.append(lax.ppermute(x, "region", swaps))
        return blocks
    everyone = lax.all_gather(x, "region", axis=0)
    me = lax.axis_index("region")
    return [
        lax.dynamic_index_in_dim(everyone, lax.rem(me + s, regions), 0, keepdims=False)
        for s in range(1, regions)
    ]


def consensus_admm(
    kkt_inverse, bus_load, bus_limit, copy_local, copy_dest, copy_slot, copy_key, own_key
):
    del copy_slot, own_key
    own = kkt_inverse[0]
    load = bus_load[0]
    regions = lax.axis_size("region")
    others = regions - 1
    half, buses = own.shape
    cols = load.shape[1]
    copies = copy_local.shape[1]
    blocks = 3 if half % (3 * copies) == 0 else 1
    small = ((copies, cols), F32)
    small16 = ((copies, cols), BF16)

    local, own, limit, load, dest, key, part = in_vmem(
        gather_kernel,
        [
            (copy_local.shape, jnp.int32), ((half, buses), BF16), (bus_limit.shape, F32),
            ((buses, cols), BF16), (copy_dest.shape, jnp.int32), (copy_key.shape, jnp.int32),
            ((copies, buses), BF16),
        ],
        from_hbm=(copy_local, own, bus_limit, load, copy_dest, copy_key),
        scratch=(pltpu.SemaphoreType.DMA((5,)), pltpu.SemaphoreType.DMA((blocks,))),
    )
    load_other = swap_row(bus_load[0])
    (theirs,) = in_vmem(theirs_kernel, [small], part, load_other)
    from_partner = swap_row(theirs)
    swapped = swap_row(own)
    other = swap_row(part)
    mine, bound_c = in_vmem(mine_kernel, [small, small], part, load, local, limit)
    at, sent, message = in_vmem(
        first_kernel,
        [small, small, ((copies + TAIL, cols), BF16)],
        mine, from_partner, bound_c, dest, key,
    )
    arrived = from_others(message, regions)
    known, known_c, block, own_sum, rows, place, bound, keep, load_c, wanted = in_vmem(
        first_solve_kernel,
        [
            ((buses, cols), BF16), small, ((copies, copies), BF16), small,
            ((copies, buses), BF16), ((buses, copies), BF16), ((buses, cols), F32),
            ((buses, cols), F32), small, ((copies, copies), F32),
        ],
        local, limit, own, swapped, load, part, other, dest, key, at,
    )
    masks, share, totals, change, drive_c, at, dual, shared, sent = in_vmem(
        functools.partial(first_mean_kernel, others),
        [((copies, others * copies), BF16), small, small, small16, small16] + [small] * 4,
        *arrived, dest, key, wanted, own_sum, at, load_c, bound_c, known_c, block, sent,
    )
    for iteration in range(1, ITERS):
        arrived = from_others(change, regions)
        if iteration < ITERS - 1:
            known, known_c, own_sum = in_vmem(
                next_solve_kernel,
                [((buses, cols), BF16), small, small],
                own, swapped, load, bound, keep, rows, place, dest, key, shared, known,
                drive_c,
            )
            more = iteration < ITERS - 2
            totals, change, drive_c, at, dual, shared, *kept = in_vmem(
                functools.partial(next_mean_kernel, others),
                [small, small16, small16] + [small] * (4 if more else 3),
                *arrived, masks, share, totals, dual, own_sum, at, load_c, bound_c, known_c,
                block, sent,
            )
            sent = kept[0] if more else None
        else:
            dispatch, own_sum = in_vmem(
                last_solve_kernel,
                [((buses, cols), F32), small],
                own, swapped, bound, place, dest, key, shared, known, drive_c,
                to_hbm=1,
                scratch=(pltpu.VMEM((buses, cols), F32), pltpu.SemaphoreType.DMA((4,))),
            )
            (dual,) = in_vmem(
                functools.partial(last_mean_kernel, others),
                [small],
                *arrived, masks, share, totals, dual, own_sum, at,
                to_hbm=1,
                scratch=(pltpu.VMEM((copies, cols), F32), pltpu.SemaphoreType.DMA),
            )
    return (dispatch[None], dual[None])


def solution(mesh):
    return jax.shard_map(
        consensus_admm,
        mesh=mesh,
        in_specs=(
            P("region", "row", None),
            P("region", None, ("batch", "scen", "row")),
            P("region", None),
            P("region", None),
            P("region", None),
            P("region", None),
            P("region", None),
            P("region", None, None),
        ),
        out_specs=(
            P("region", None, ("batch", "scen", "row")),
            P("region", None, ("batch", "scen", "row")),
        ),
        check_vma=False,
    )
```

```python
import functools

import jax
import jax.numpy as jnp
from jax import lax
from jax.experimental import pallas as pl
from jax.experimental.pallas import tpu as pltpu
from jax.sharding import PartitionSpec as P

GO = 64
ITERS = 3
PENALTY = 1.0
PROXIMAL = 0.5
TAIL = 16
F32 = jnp.float32
BF16 = jnp.bfloat16
VMEM = pl.BlockSpec(memory_space=pltpu.VMEM)


def dot32(a, b, precision=None):
    return jnp.dot(a, b, precision=precision, preferred_element_type=F32)


def in_vmem(body, outs, *operands, to_hbm=0, from_hbm=(), scratch=()):
    anywhere = pl.BlockSpec(memory_space=pl.ANY)
    return pl.pallas_call(
        body,
        out_shape=[
            jax.ShapeDtypeStruct(*out) if n < to_hbm else pltpu.VMEM(*out)
            for n, out in enumerate(outs)
        ],
        in_specs=[anywhere] * len(from_hbm) + [VMEM] * len(operands),
        out_specs=[anywhere if n < to_hbm else VMEM for n in range(len(outs))],
        scratch_shapes=list(scratch),
        compiler_params=pltpu.CompilerParams(vmem_limit_bytes=12 << 20),
    )(
        *[pltpu.with_memory_space_constraint(x, pltpu.HBM) for x in from_hbm],
        *[pltpu.with_memory_space_constraint(x, pltpu.VMEM) for x in operands],
    )


def column(row):
    size = row.shape[1]
    return jnp.broadcast_to(row.astype(F32), (size, size)).T


def lanes(shape, offset=0):
    return (lax.broadcasted_iota(jnp.int32, shape, 1) + offset).astype(F32)


def ones_where(condition):
    return jnp.where(condition, 1.0, 0.0).astype(BF16)


def half_starts(half):
    first = lax.axis_index("row") * half
    return first, half - first


def gather_kernel(
    local_hbm, inverse_hbm, limit_hbm, load_hbm, dest_hbm, key_hbm,
    local_ref, own_ref, limit_ref, load_ref, dest_ref, key_ref, part_ref, small_sems,
    chunk_sems,
):
    copies = local_ref.shape[1]
    half = own_ref.shape[0]
    size = half // chunk_sems.shape[0]
    first = pltpu.make_async_copy(local_hbm, local_ref, small_sems.at[0])
    first.start()
    pieces = []
    for c in range(chunk_sems.shape[0]):
        block = slice(c * size, (c + 1) * size)
        pieces.append(
            pltpu.make_async_copy(inverse_hbm.at[block], own_ref.at[block], chunk_sems.at[c])
        )
        pieces[c].start()
    rest = [
        pltpu.make_async_copy(source, target, small_sems.at[n + 1])
        for n, (source, target) in enumerate(
            ((load_hbm, load_ref), (limit_hbm, limit_ref), (dest_hbm, dest_ref), (key_hbm, key_ref))
        )
    ]
    for copy in rest:
        copy.start()
    first.wait()
    wanted = column(local_ref[...]) - (lax.axis_index("row") * half).astype(F32)
    found = jnp.zeros(part_ref.shape, BF16)
    for c, piece in enumerate(pieces):
        hits = [
            ones_where(wanted == lanes(wanted.shape, column_start))
            for column_start in range(c * size, (c + 1) * size, copies)
        ]
        piece.wait()
        block = own_ref[c * size:(c + 1) * size, :]
        found = found + dot32(jnp.concatenate(hits, 1), block).astype(BF16)
    part_ref[...] = found
    for copy in rest:
        copy.wait()


def mine_kernel(part_ref, load_ref, local_ref, limit_ref, mine_ref, bound_c_ref):
    mine_ref[...] = dot32(part_ref[...], load_ref[...])
    wanted = column(local_ref[...])
    copies = wanted.shape[0]
    limits = jnp.zeros(wanted.shape, F32)
    for c in range(0, limit_ref.shape[1], copies):
        hit = wanted == lanes(wanted.shape, c)
        limits = limits + jnp.where(hit, limit_ref[:, c:c + copies], 0.0)
    bound_c_ref[...] = jnp.broadcast_to(jnp.sum(limits, 1, keepdims=True), bound_c_ref.shape)


def tables(local_ref, limit_ref, load_ref, place_ref, bound_ref, keep_ref, load_c_ref):
    buses, cols = load_ref.shape
    local = local_ref[...]
    copies = local.shape[1]
    place = ones_where(lax.broadcasted_iota(jnp.int32, (buses, copies), 0) == local)
    place_ref[...] = place
    keep_ref[...] = 1.0 - dot32(place, jnp.ones((copies, cols), BF16))
    wanted = column(local)
    picks = []
    for c in range(0, buses, copies):
        limit = limit_ref[:, c:c + copies]
        bound_ref[c:c + copies, :] = jnp.broadcast_to(limit, (cols, copies)).T
        picks.append(ones_where(wanted == lanes(wanted.shape, c)))
    load_c_ref[...] = dot32(jnp.concatenate(picks, 1), load_ref[...])


def theirs_kernel(part_ref, load_other_ref, theirs_ref):
    theirs_ref[...] = dot32(part_ref[...], load_other_ref[...])


def first_kernel(
    mine_ref, from_partner_ref, bound_c_ref, dest_ref, key_ref, at_ref, sent_ref, message_ref
):
    bound = bound_c_ref[...]
    at = jnp.clip(mine_ref[...] + from_partner_ref[...], -bound, bound)
    at_ref[...] = at
    copies, cols = at.shape
    message = at.astype(BF16)
    sent_ref[...] = message.astype(F32)
    message_ref[:copies, :] = message
    line = lax.broadcasted_iota(jnp.int32, (TAIL, cols), 0)
    ids = jnp.where(line == 0, dest_ref[...], jnp.where(line == 1, key_ref[...], 0))
    message_ref[copies:, :] = ids.astype(F32).astype(BF16)


def own_ids(dest_ref, key_ref):
    return (dest_ref[...] * GO + key_ref[...]).astype(F32)


def own_total(dest_ref, key_ref, shared_ref):
    ids = own_ids(dest_ref, key_ref)
    mine = jnp.where(column(ids) == ids, 1.0, 0.0)
    return dot32(mine, shared_ref[...], lax.Precision.HIGHEST)


def solve_all(own_ref, swapped_ref, drive, bound_ref):
    half = own_ref.shape[0]
    piece = half // 4
    for start, part_ref in zip(half_starts(half), (own_ref, swapped_ref)):
        for step in range(0, half, piece):
            rows = pl.ds(pl.multiple_of(start + step, piece), piece)
            bound = bound_ref[rows, :]
            solved = dot32(part_ref[step:step + piece, :], drive)
            yield rows, jnp.clip(solved, -bound, bound)


def known_part(
    own_ref, swapped_ref, drive, bound_ref, keep_ref, load_ref, rows_ref, known_ref, known_c_ref
):
    for rows, dispatch in solve_all(own_ref, swapped_ref, drive, bound_ref):
        known = (load_ref[rows, :].astype(F32) + PROXIMAL * dispatch) * keep_ref[rows, :]
        known_ref[rows, :] = known.astype(BF16)
    known_c_ref[...] = dot32(rows_ref[...], known_ref[...])


def first_solve_kernel(
    local_ref, limit_ref, own_ref, swapped_ref, load_ref, part_ref, other_ref, dest_ref, key_ref,
    shared_ref, known_ref, known_c_ref, block_ref, own_total_ref, rows_ref, place_ref, bound_ref,
    keep_ref, load_c_ref, wanted_ref,
):
    tables(local_ref, limit_ref, load_ref, place_ref, bound_ref, keep_ref, load_c_ref)
    rows_ref[...] = (part_ref[...].astype(F32) + other_ref[...].astype(F32)).astype(BF16)
    wanted_ref[...] = column(own_ids(dest_ref, key_ref))
    own_total_ref[...] = own_total(dest_ref, key_ref, shared_ref)
    block_ref[...] = dot32(rows_ref[...], place_ref[...]).astype(BF16)
    known_part(
        own_ref, swapped_ref, load_ref[...], bound_ref, keep_ref, load_ref, rows_ref, known_ref,
        known_c_ref,
    )


def drive_of(known_ref, place_ref, drive_c_ref):
    return known_ref[...] + dot32(place_ref[...], drive_c_ref[...]).astype(BF16)


def next_solve_kernel(
    own_ref, swapped_ref, load_ref, bound_ref, keep_ref, rows_ref, place_ref, dest_ref, key_ref,
    shared_ref, before_ref, drive_c_ref, known_ref, known_c_ref, own_total_ref,
):
    own_total_ref[...] = own_total(dest_ref, key_ref, shared_ref)
    drive = drive_of(before_ref, place_ref, drive_c_ref)
    known_part(
        own_ref, swapped_ref, drive, bound_ref, keep_ref, load_ref, rows_ref, known_ref,
        known_c_ref,
    )


def last_solve_kernel(
    own_ref, swapped_ref, bound_ref, place_ref, dest_ref, key_ref, shared_ref, before_ref,
    drive_c_ref, dispatch_hbm, own_total_ref, dispatch_ref, sems,
):
    drive = drive_of(before_ref, place_ref, drive_c_ref)
    writes = []
    for rows, dispatch in solve_all(own_ref, swapped_ref, drive, bound_ref):
        dispatch_ref[rows, :] = dispatch
        writes.append(
            pltpu.make_async_copy(
                dispatch_ref.at[rows, :], dispatch_hbm.at[rows, :], sems.at[len(writes)]
            )
        )
        writes[-1].start()
    own_total_ref[...] = own_total(dest_ref, key_ref, shared_ref)
    for write in writes:
        write.wait()


def advance(
    consensus, dual, at_ref, load_c_ref, bound_c_ref, known_c_ref, block_ref, sent_ref, change_ref,
    drive_c_ref, at_out_ref, dual_out_ref, shared_ref, *sent_out_ref,
):
    at = at_ref[...]
    dual = dual + at - consensus
    boundary = consensus - dual
    drive_c = (load_c_ref[...] + PROXIMAL * at + PENALTY * boundary).astype(BF16)
    bound = bound_c_ref[...]
    at = jnp.clip(known_c_ref[...] + dot32(block_ref[...], drive_c), -bound, bound)
    shared = at + dual
    sent = sent_ref[...]
    change = (shared - sent).astype(BF16)
    change_ref[...] = change
    for ref in sent_out_ref:
        ref[...] = sent + change.astype(F32)
    drive_c_ref[...] = drive_c
    at_out_ref[...] = at
    dual_out_ref[...] = dual
    shared_ref[...] = shared


def first_mean_kernel(others, *refs):
    blocks, refs = refs[:others], refs[others:]
    (dest_ref, key_ref, wanted_ref, own_total_ref, at_ref, load_c_ref, bound_c_ref, known_c_ref,
     block_ref, sent_ref), refs = refs[:10], refs[10:]
    masks_ref, share_ref, totals_ref = refs[:3]
    ids = own_ids(dest_ref, key_ref)
    copies = ids.shape[1]
    wanted = wanted_ref[...]
    count = jnp.where(wanted == ids, 1.0, 0.0)
    masks = []
    for block in blocks:
        theirs = block[copies:copies + 2, :].astype(F32)
        mask = jnp.where(wanted == theirs[0:1] * GO + theirs[1:2], 1.0, 0.0)
        count = count + mask
        masks.append(mask.astype(BF16))
    mask = jnp.concatenate(masks, 1)
    masks_ref[...] = mask
    share = 1.0 / jnp.maximum(jnp.sum(count, 1, keepdims=True), 1.0)
    share = jnp.broadcast_to(share, share_ref.shape)
    share_ref[...] = share
    totals = dot32(mask, jnp.concatenate([block[:copies, :] for block in blocks], 0))
    totals_ref[...] = totals
    consensus = (own_total_ref[...] + totals) * share
    advance(
        consensus, 0.0, at_ref, load_c_ref, bound_c_ref, known_c_ref, block_ref, sent_ref,
        *refs[3:],
    )


def others_total(blocks, masks_ref, totals_ref):
    arrived = jnp.concatenate([block[...] for block in blocks], 0)
    return totals_ref[...] + dot32(masks_ref[...], arrived)


def next_mean_kernel(others, *refs):
    blocks, refs = refs[:others], refs[others:]
    (masks_ref, share_ref, totals_ref, dual_ref, own_total_ref, at_ref, load_c_ref, bound_c_ref,
     known_c_ref, block_ref, sent_ref), refs = refs[:11], refs[11:]
    totals = others_total(blocks, masks_ref, totals_ref)
    refs[0][...] = totals
    consensus = (own_total_ref[...] + totals) * share_ref[...]
    advance(
        consensus, dual_ref[...], at_ref, load_c_ref, bound_c_ref, known_c_ref, block_ref,
        sent_ref, *refs[1:],
    )


def last_mean_kernel(others, *refs):
    blocks, refs = refs[:others], refs[others:]
    masks_ref, share_ref, totals_ref, dual_ref, own_total_ref, at_ref, out_hbm, out_ref, sem = refs
    totals = others_total(blocks, masks_ref, totals_ref)
    consensus = (own_total_ref[...] + totals) * share_ref[...]
    out_ref[...] = dual_ref[...] + at_ref[...] - consensus
    write = pltpu.make_async_copy(out_ref, out_hbm, sem)
    write.start()
    write.wait()


def swap_row(x):
    return lax.ppermute(x, "row", [(0, 1), (1, 0)])


def from_others(x, regions):
    paired = regions & (regions - 1) == 0
    blocks = []
    for s in range(1, regions):
        targets = [(i, i ^ s if paired else (i + s) % regions) for i in range(regions)]
        blocks.append(lax.ppermute(x, "region", targets))
    return blocks


def consensus_admm(
    kkt_inverse, bus_load, bus_limit, copy_local, copy_dest, copy_slot, copy_key, own_key
):
    del copy_slot, own_key
    own = kkt_inverse[0]
    load = bus_load[0]
    regions = lax.axis_size("region")
    others = regions - 1
    half, buses = own.shape
    cols = load.shape[1]
    copies = copy_local.shape[1]
    blocks = 3 if half % (3 * copies) == 0 else 1
    small = ((copies, cols), F32)
    small16 = ((copies, cols), BF16)

    local, own, limit, load, dest, key, part = in_vmem(
        gather_kernel,
        [
            (copy_local.shape, jnp.int32), ((half, buses), BF16), (bus_limit.shape, F32),
            ((buses, cols), BF16), (copy_dest.shape, jnp.int32), (copy_key.shape, jnp.int32),
            ((copies, buses), BF16),
        ],
        from_hbm=(copy_local, own, bus_limit, load, copy_dest, copy_key),
        scratch=(pltpu.SemaphoreType.DMA((5,)), pltpu.SemaphoreType.DMA((blocks,))),
    )
    load_other = swap_row(bus_load[0])
    (theirs,) = in_vmem(theirs_kernel, [small], part, load_other)
    from_partner = swap_row(theirs)
    swapped = swap_row(own)
    other = swap_row(part)
    mine, bound_c = in_vmem(mine_kernel, [small, small], part, load, local, limit)
    at, sent, message = in_vmem(
        first_kernel,
        [small, small, ((copies + TAIL, cols), BF16)],
        mine, from_partner, bound_c, dest, key,
    )
    arrived = from_others(message, regions)
    known, known_c, block, own_sum, rows, place, bound, keep, load_c, wanted = in_vmem(
        first_solve_kernel,
        [
            ((buses, cols), BF16), small, ((copies, copies), BF16), small,
            ((copies, buses), BF16), ((buses, copies), BF16), ((buses, cols), F32),
            ((buses, cols), F32), small, ((copies, copies), F32),
        ],
        local, limit, own, swapped, load, part, other, dest, key, at,
    )
    masks, share, totals, change, drive_c, at, dual, shared, sent = in_vmem(
        functools.partial(first_mean_kernel, others),
        [((copies, others * copies), BF16), small, small, small16, small16] + [small] * 4,
        *arrived, dest, key, wanted, own_sum, at, load_c, bound_c, known_c, block, sent,
    )
    for iteration in range(1, ITERS):
        arrived = from_others(change, regions)
        if iteration < ITERS - 1:
            known, known_c, own_sum = in_vmem(
                next_solve_kernel,
                [((buses, cols), BF16), small, small],
                own, swapped, load, bound, keep, rows, place, dest, key, shared, known,
                drive_c,
            )
            more = iteration < ITERS - 2
            totals, change, drive_c, at, dual, shared, *kept = in_vmem(
                functools.partial(next_mean_kernel, others),
                [small, small16, small16] + [small] * (4 if more else 3),
                *arrived, masks, share, totals, dual, own_sum, at, load_c, bound_c, known_c,
                block, sent,
            )
            sent = kept[0] if more else None
        else:
            dispatch, own_sum = in_vmem(
                last_solve_kernel,
                [((buses, cols), F32), small],
                own, swapped, bound, place, dest, key, shared, known, drive_c,
                to_hbm=1,
                scratch=(pltpu.VMEM((buses, cols), F32), pltpu.SemaphoreType.DMA((8,))),
            )
            (dual,) = in_vmem(
                functools.partial(last_mean_kernel, others),
                [small],
                *arrived, masks, share, totals, dual, own_sum, at,
                to_hbm=1,
                scratch=(pltpu.VMEM((copies, cols), F32), pltpu.SemaphoreType.DMA),
            )
    return (dispatch[None], dual[None])


def solution(mesh):
    return jax.shard_map(
        consensus_admm,
        mesh=mesh,
        in_specs=(
            P("region", "row", None),
            P("region", None, ("batch", "scen", "row")),
            P("region", None),
            P("region", None),
            P("region", None),
            P("region", None),
            P("region", None),
            P("region", None, None),
        ),
        out_specs=(
            P("region", None, ("batch", "scen", "row")),
            P("region", None, ("batch", "scen", "row")),
        ),
        check_vma=False,
    )
```

```python
import functools

import jax
import jax.numpy as jnp
from jax import lax
from jax.experimental import pallas as pl
from jax.experimental.pallas import tpu as pltpu
from jax.sharding import PartitionSpec as P

GO = 64
ITERS = 3
PENALTY = 1.0
PROXIMAL = 0.5
TAIL = 16
F32 = jnp.float32
BF16 = jnp.bfloat16
VMEM = pl.BlockSpec(memory_space=pltpu.VMEM)


def dot32(a, b, precision=None):
    return jnp.dot(a, b, precision=precision, preferred_element_type=F32)


def in_vmem(body, outs, *operands, to_hbm=0, from_hbm=(), scratch=()):
    anywhere = pl.BlockSpec(memory_space=pl.ANY)
    return pl.pallas_call(
        body,
        out_shape=[
            jax.ShapeDtypeStruct(*out) if n < to_hbm else pltpu.VMEM(*out)
            for n, out in enumerate(outs)
        ],
        in_specs=[anywhere] * len(from_hbm) + [VMEM] * len(operands),
        out_specs=[anywhere if n < to_hbm else VMEM for n in range(len(outs))],
        scratch_shapes=list(scratch),
        compiler_params=pltpu.CompilerParams(vmem_limit_bytes=12 << 20),
    )(
        *[pltpu.with_memory_space_constraint(x, pltpu.HBM) for x in from_hbm],
        *[pltpu.with_memory_space_constraint(x, pltpu.VMEM) for x in operands],
    )


def column(row):
    size = row.shape[1]
    return jnp.broadcast_to(row.astype(F32), (size, size)).T


def lanes(shape, offset=0):
    return (lax.broadcasted_iota(jnp.int32, shape, 1) + offset).astype(F32)


def ones_where(condition):
    return jnp.where(condition, 1.0, 0.0).astype(BF16)


def half_starts(half):
    first = lax.axis_index("row") * half
    return first, half - first


def gather_kernel(
    local_hbm, inverse_hbm, limit_hbm, dest_hbm, key_hbm,
    local_ref, own_ref, limit_ref, dest_ref, key_ref, part_ref, small_sems,
    chunk_sems,
):
    copies = local_ref.shape[1]
    half = own_ref.shape[0]
    size = half // chunk_sems.shape[0]
    first = pltpu.make_async_copy(local_hbm, local_ref, small_sems.at[0])
    first.start()
    pieces = []
    for c in range(chunk_sems.shape[0]):
        block = slice(c * size, (c + 1) * size)
        pieces.append(
            pltpu.make_async_copy(inverse_hbm.at[block], own_ref.at[block], chunk_sems.at[c])
        )
        pieces[c].start()
    rest = [
        pltpu.make_async_copy(source, target, small_sems.at[n + 1])
        for n, (source, target) in enumerate(
            ((limit_hbm, limit_ref), (dest_hbm, dest_ref), (key_hbm, key_ref))
        )
    ]
    for copy in rest:
        copy.start()
    first.wait()
    wanted = column(local_ref[...]) - (lax.axis_index("row") * half).astype(F32)
    found = jnp.zeros(part_ref.shape, BF16)
    for c, piece in enumerate(pieces):
        hits = [
            ones_where(wanted == lanes(wanted.shape, column_start))
            for column_start in range(c * size, (c + 1) * size, copies)
        ]
        piece.wait()
        block = own_ref[c * size:(c + 1) * size, :]
        found = found + dot32(jnp.concatenate(hits, 1), block).astype(BF16)
    part_ref[...] = found
    for copy in rest:
        copy.wait()


def mine_kernel(part_ref, load_ref, local_ref, limit_ref, mine_ref, bound_c_ref):
    mine_ref[...] = dot32(part_ref[...], load_ref[...])
    wanted = column(local_ref[...])
    copies = wanted.shape[0]
    limits = jnp.zeros(wanted.shape, F32)
    for c in range(0, limit_ref.shape[1], copies):
        hit = wanted == lanes(wanted.shape, c)
        limits = limits + jnp.where(hit, limit_ref[:, c:c + copies], 0.0)
    bound_c_ref[...] = jnp.broadcast_to(jnp.sum(limits, 1, keepdims=True), bound_c_ref.shape)


def tables(local_ref, limit_ref, load_ref, place_ref, bound_ref, keep_ref, load_c_ref):
    buses, cols = load_ref.shape
    local = local_ref[...]
    copies = local.shape[1]
    place = ones_where(lax.broadcasted_iota(jnp.int32, (buses, copies), 0) == local)
    place_ref[...] = place
    keep_ref[...] = 1.0 - dot32(place, jnp.ones((copies, cols), BF16))
    wanted = column(local)
    picks = []
    for c in range(0, buses, copies):
        limit = limit_ref[:, c:c + copies]
        bound_ref[c:c + copies, :] = jnp.broadcast_to(limit, (cols, copies)).T
        picks.append(ones_where(wanted == lanes(wanted.shape, c)))
    load_c_ref[...] = dot32(jnp.concatenate(picks, 1), load_ref[...])


def theirs_kernel(part_ref, load_other_ref, theirs_ref):
    theirs_ref[...] = dot32(part_ref[...], load_other_ref[...])


def first_kernel(
    mine_ref, from_partner_ref, bound_c_ref, dest_ref, key_ref, at_ref, sent_ref, message_ref
):
    bound = bound_c_ref[...]
    at = jnp.clip(mine_ref[...] + from_partner_ref[...], -bound, bound)
    at_ref[...] = at
    copies, cols = at.shape
    message = at.astype(BF16)
    sent_ref[...] = message.astype(F32)
    message_ref[:copies, :] = message
    line = lax.broadcasted_iota(jnp.int32, (TAIL, cols), 0)
    ids = jnp.where(line == 0, dest_ref[...], jnp.where(line == 1, key_ref[...], 0))
    message_ref[copies:, :] = ids.astype(F32).astype(BF16)


def own_ids(dest_ref, key_ref):
    return (dest_ref[...] * GO + key_ref[...]).astype(F32)


def own_total(dest_ref, key_ref, shared_ref):
    ids = own_ids(dest_ref, key_ref)
    mine = jnp.where(column(ids) == ids, 1.0, 0.0)
    return dot32(mine, shared_ref[...], lax.Precision.HIGHEST)


def solve_all(own_ref, swapped_ref, drive, bound_ref):
    half = own_ref.shape[0]
    piece = half // 4
    for start, part_ref in zip(half_starts(half), (own_ref, swapped_ref)):
        for step in range(0, half, piece):
            rows = pl.ds(pl.multiple_of(start + step, piece), piece)
            bound = bound_ref[rows, :]
            solved = dot32(part_ref[step:step + piece, :], drive)
            yield rows, jnp.clip(solved, -bound, bound)


def known_part(
    own_ref, swapped_ref, drive, bound_ref, keep_ref, load_ref, rows_ref, known_ref, known_c_ref
):
    for rows, dispatch in solve_all(own_ref, swapped_ref, drive, bound_ref):
        known = (load_ref[rows, :].astype(F32) + PROXIMAL * dispatch) * keep_ref[rows, :]
        known_ref[rows, :] = known.astype(BF16)
    known_c_ref[...] = dot32(rows_ref[...], known_ref[...])


def first_solve_kernel(
    local_ref, limit_ref, own_ref, swapped_ref, load_ref, part_ref, other_ref, dest_ref, key_ref,
    shared_ref, known_ref, known_c_ref, block_ref, own_total_ref, rows_ref, place_ref, bound_ref,
    keep_ref, load_c_ref, wanted_ref,
):
    tables(local_ref, limit_ref, load_ref, place_ref, bound_ref, keep_ref, load_c_ref)
    rows_ref[...] = (part_ref[...].astype(F32) + other_ref[...].astype(F32)).astype(BF16)
    wanted_ref[...] = column(own_ids(dest_ref, key_ref))
    own_total_ref[...] = own_total(dest_ref, key_ref, shared_ref)
    block_ref[...] = dot32(rows_ref[...], place_ref[...]).astype(BF16)
    known_part(
        own_ref, swapped_ref, load_ref[...], bound_ref, keep_ref, load_ref, rows_ref, known_ref,
        known_c_ref,
    )


def drive_of(known_ref, place_ref, drive_c_ref):
    return known_ref[...] + dot32(place_ref[...], drive_c_ref[...]).astype(BF16)


def next_solve_kernel(
    own_ref, swapped_ref, load_ref, bound_ref, keep_ref, rows_ref, place_ref, dest_ref, key_ref,
    shared_ref, before_ref, drive_c_ref, known_ref, known_c_ref, own_total_ref,
):
    own_total_ref[...] = own_total(dest_ref, key_ref, shared_ref)
    drive = drive_of(before_ref, place_ref, drive_c_ref)
    known_part(
        own_ref, swapped_ref, drive, bound_ref, keep_ref, load_ref, rows_ref, known_ref,
        known_c_ref,
    )


def last_solve_kernel(
    own_ref, swapped_ref, bound_ref, place_ref, dest_ref, key_ref, shared_ref, before_ref,
    drive_c_ref, dispatch_hbm, own_total_ref, dispatch_ref, sems,
):
    drive = drive_of(before_ref, place_ref, drive_c_ref)
    writes = []
    for rows, dispatch in solve_all(own_ref, swapped_ref, drive, bound_ref):
        dispatch_ref[rows, :] = dispatch
        writes.append(
            pltpu.make_async_copy(
                dispatch_ref.at[rows, :], dispatch_hbm.at[rows, :], sems.at[len(writes)]
            )
        )
        writes[-1].start()
    own_total_ref[...] = own_total(dest_ref, key_ref, shared_ref)
    for write in writes:
        write.wait()


def advance(
    consensus, dual, at_ref, load_c_ref, bound_c_ref, known_c_ref, block_ref, sent_ref, change_ref,
    drive_c_ref, at_out_ref, dual_out_ref, shared_ref, *sent_out_ref,
):
    at = at_ref[...]
    dual = dual + at - consensus
    boundary = consensus - dual
    drive_c = (load_c_ref[...] + PROXIMAL * at + PENALTY * boundary).astype(BF16)
    bound = bound_c_ref[...]
    at = jnp.clip(known_c_ref[...] + dot32(block_ref[...], drive_c), -bound, bound)
    shared = at + dual
    sent = sent_ref[...]
    change = (shared - sent).astype(BF16)
    change_ref[...] = change
    for ref in sent_out_ref:
        ref[...] = sent + change.astype(F32)
    drive_c_ref[...] = drive_c
    at_out_ref[...] = at
    dual_out_ref[...] = dual
    shared_ref[...] = shared


def first_mean_kernel(others, *refs):
    blocks, refs = refs[:others], refs[others:]
    (dest_ref, key_ref, wanted_ref, own_total_ref, at_ref, load_c_ref, bound_c_ref, known_c_ref,
     block_ref, sent_ref), refs = refs[:10], refs[10:]
    masks_ref, share_ref, totals_ref = refs[:3]
    ids = own_ids(dest_ref, key_ref)
    copies = ids.shape[1]
    wanted = wanted_ref[...]
    count = jnp.where(wanted == ids, 1.0, 0.0)
    masks = []
    for block in blocks:
        theirs = block[copies:copies + 2, :].astype(F32)
        mask = jnp.where(wanted == theirs[0:1] * GO + theirs[1:2], 1.0, 0.0)
        count = count + mask
        masks.append(mask.astype(BF16))
    mask = jnp.concatenate(masks, 1)
    masks_ref[...] = mask
    share = 1.0 / jnp.maximum(jnp.sum(count, 1, keepdims=True), 1.0)
    share = jnp.broadcast_to(share, share_ref.shape)
    share_ref[...] = share
    totals = dot32(mask, jnp.concatenate([block[:copies, :] for block in blocks], 0))
    totals_ref[...] = totals
    consensus = (own_total_ref[...] + totals) * share
    advance(
        consensus, 0.0, at_ref, load_c_ref, bound_c_ref, known_c_ref, block_ref, sent_ref,
        *refs[3:],
    )


def others_total(blocks, masks_ref, totals_ref):
    arrived = jnp.concatenate([block[...] for block in blocks], 0)
    return totals_ref[...] + dot32(masks_ref[...], arrived)


def next_mean_kernel(others, *refs):
    blocks, refs = refs[:others], refs[others:]
    (masks_ref, share_ref, totals_ref, dual_ref, own_total_ref, at_ref, load_c_ref, bound_c_ref,
     known_c_ref, block_ref, sent_ref), refs = refs[:11], refs[11:]
    totals = others_total(blocks, masks_ref, totals_ref)
    refs[0][...] = totals
    consensus = (own_total_ref[...] + totals) * share_ref[...]
    advance(
        consensus, dual_ref[...], at_ref, load_c_ref, bound_c_ref, known_c_ref, block_ref,
        sent_ref, *refs[1:],
    )


def last_mean_kernel(others, *refs):
    blocks, refs = refs[:others], refs[others:]
    masks_ref, share_ref, totals_ref, dual_ref, own_total_ref, at_ref, out_hbm, out_ref, sem = refs
    totals = others_total(blocks, masks_ref, totals_ref)
    consensus = (own_total_ref[...] + totals) * share_ref[...]
    out_ref[...] = dual_ref[...] + at_ref[...] - consensus
    write = pltpu.make_async_copy(out_ref, out_hbm, sem)
    write.start()
    write.wait()


def swap_row(x):
    return lax.ppermute(x, "row", [(0, 1), (1, 0)])


def from_others(x, regions):
    paired = regions & (regions - 1) == 0
    blocks = []
    for s in range(1, regions):
        targets = [(i, i ^ s if paired else (i + s) % regions) for i in range(regions)]
        blocks.append(lax.ppermute(x, "region", targets))
    return blocks


def consensus_admm(
    kkt_inverse, bus_load, bus_limit, copy_local, copy_dest, copy_slot, copy_key, own_key
):
    del copy_slot, own_key
    own = kkt_inverse[0]
    load = bus_load[0]
    regions = lax.axis_size("region")
    others = regions - 1
    half, buses = own.shape
    cols = load.shape[1]
    copies = copy_local.shape[1]
    blocks = 2 if half % (2 * copies) == 0 else 1
    small = ((copies, cols), F32)
    small16 = ((copies, cols), BF16)

    local, own, limit, dest, key, part = in_vmem(
        gather_kernel,
        [
            (copy_local.shape, jnp.int32), ((half, buses), BF16), (bus_limit.shape, F32),
            (copy_dest.shape, jnp.int32), (copy_key.shape, jnp.int32),
            ((copies, buses), BF16),
        ],
        from_hbm=(copy_local, own, bus_limit, copy_dest, copy_key),
        scratch=(pltpu.SemaphoreType.DMA((4,)), pltpu.SemaphoreType.DMA((blocks,))),
    )
    load_other = swap_row(bus_load[0])
    (theirs,) = in_vmem(theirs_kernel, [small], part, load_other)
    from_partner = swap_row(theirs)
    swapped = swap_row(own)
    other = swap_row(part)
    mine, bound_c = in_vmem(mine_kernel, [small, small], part, load, local, limit)
    at, sent, message = in_vmem(
        first_kernel,
        [small, small, ((copies + TAIL, cols), BF16)],
        mine, from_partner, bound_c, dest, key,
    )
    arrived = from_others(message, regions)
    known, known_c, block, own_sum, rows, place, bound, keep, load_c, wanted = in_vmem(
        first_solve_kernel,
        [
            ((buses, cols), BF16), small, ((copies, copies), BF16), small,
            ((copies, buses), BF16), ((buses, copies), BF16), ((buses, cols), F32),
            ((buses, cols), F32), small, ((copies, copies), F32),
        ],
        local, limit, own, swapped, load, part, other, dest, key, at,
    )
    masks, share, totals, change, drive_c, at, dual, shared, sent = in_vmem(
        functools.partial(first_mean_kernel, others),
        [((copies, others * copies), BF16), small, small, small16, small16] + [small] * 4,
        *arrived, dest, key, wanted, own_sum, at, load_c, bound_c, known_c, block, sent,
    )
    for iteration in range(1, ITERS):
        arrived = from_others(change, regions)
        if iteration < ITERS - 1:
            known, known_c, own_sum = in_vmem(
                next_solve_kernel,
                [((buses, cols), BF16), small, small],
                own, swapped, load, bound, keep, rows, place, dest, key, shared, known,
                drive_c,
            )
            more = iteration < ITERS - 2
            totals, change, drive_c, at, dual, shared, *kept = in_vmem(
                functools.partial(next_mean_kernel, others),
                [small, small16, small16] + [small] * (4 if more else 3),
                *arrived, masks, share, totals, dual, own_sum, at, load_c, bound_c, known_c,
                block, sent,
            )
            sent = kept[0] if more else None
        else:
            dispatch, own_sum = in_vmem(
                last_solve_kernel,
                [((buses, cols), F32), small],
                own, swapped, bound, place, dest, key, shared, known, drive_c,
                to_hbm=1,
                scratch=(pltpu.VMEM((buses, cols), F32), pltpu.SemaphoreType.DMA((8,))),
            )
            (dual,) = in_vmem(
                functools.partial(last_mean_kernel, others),
                [small],
                *arrived, masks, share, totals, dual, own_sum, at,
                to_hbm=1,
                scratch=(pltpu.VMEM((copies, cols), F32), pltpu.SemaphoreType.DMA),
            )
    return (dispatch[None], dual[None])


def solution(mesh):
    return jax.shard_map(
        consensus_admm,
        mesh=mesh,
        in_specs=(
            P("region", "row", None),
            P("region", None, ("batch", "scen", "row")),
            P("region", None),
            P("region", None),
            P("region", None),
            P("region", None),
            P("region", None),
            P("region", None, None),
        ),
        out_specs=(
            P("region", None, ("batch", "scen", "row")),
            P("region", None, ("batch", "scen", "row")),
        ),
        check_vma=False,
    )
```
